32 devices in a mesh: wide: 8 (over z, y), narrow: 4 (over x, core).
Axes of the slice: x: 2, y: 2, z: 4, core: 2. Of those that a mesh axis runs over, the one named last changes fastest.
Arguments:
- activations: bfloat16 [256, 28672], P('wide', 'narrow'), may hold values from -6 to 6
- out_grads: bfloat16 [256, 8192], P('wide'), may hold values from -6 to 6
- basis_in: bfloat16 [28672, 28672], P('narrow', 'wide'), may hold values from -0.03125 to 0.03125
- basis_out: bfloat16 [8192, 8192], P('wide', 'narrow'), may hold values from -0.0625 to 0.0625
- eigenvalues: bfloat16 [8192, 28672], P('narrow', 'wide'), may hold values from 0.29882812 to 10
- queries: bfloat16 [2, 8192, 28672], P(None, 'narrow', 'wide'), may hold values from -0.00036621094 to 0.00036621094
- doc_ids: int32 [256], replicated, may hold values from 0 to 15, never falling along the last dimension, each value on 1 to 32 neighbouring positions
Outputs:
- scores: float32 [16, 2], replicated
The draws below stay inside these ranges and needn't reach their ends.
Inputs may be any that keep to these rules, and one draw needn't show every extreme that they name: `doc_ids`: document numbers never fall along the tokens; each document has 1 to 32 tokens.
All inputs are finite; a program needn't handle non-finite values.
Results may differ from the reference program's by a relative error of at most 0.0051.
Values may be sent and summed in bfloat16 or wider, within the bound.
A program may use at most 192 MiB of HBM per device.

```python
import math
import jax
import jax.numpy as jnp
import numpy as np
from jax import lax

D = 8192
FF = 28672
NQ = 2
TOKENS = 256
DOCS = 16
DOC_MOST = 32


def shard_levels(stream_key, dims, split, smallest, largest):
    level = 1.0
    for position, shards_of in split:
        heights = jax.random.uniform(jax.random.fold_in(jax.random.fold_in(stream_key, 6), position), (shards_of,), jnp.float32, smallest / len(split), largest / len(split))
        level = level * jnp.repeat(jnp.exp(heights), dims[position] // shards_of).reshape((-1,) + (1,) * (len(dims) - 1 - position))
    return level


def profile(number_of, total, bound, skew):
    loads = [(1 << 20) // math.isqrt(standing ** skew) + 1 for standing in range(2, number_of + 1)]
    rest, counts = total - bound - (number_of - 1), [1] * (number_of - 1)
    while rest > 0:
        candidates = [i for i in range(number_of - 1) if counts[i] < bound]
        pool, budget = sum([loads[i] for i in candidates]), rest
        for i in candidates:
            extra = min(bound - counts[i], max(1, budget * loads[i] // pool), rest)
            counts[i] = counts[i] + extra
            rest = rest - extra
    return np.array([bound] + counts)


def uneven(stream_key, number_of, total, bound, slope):
    if number_of == 2:
        one = jax.random.randint(stream_key, (), max(1, total - bound), min(bound, total - 1) + 1)
        return jnp.stack([one, total - one])
    lengths = jnp.asarray(profile(number_of, total, bound, slope), jnp.int32)
    couples = (number_of - 1) // 2
    donor, sink = lengths[1:1 + 2 * couples:2], lengths[2:2 + 2 * couples:2]
    margin = jnp.minimum(donor - 1, bound - sink)
    passed = jax.random.randint(jax.random.fold_in(stream_key, 1), (couples,), 0, 1 << 20) % (margin + 1)
    lengths = lengths.at[1:1 + 2 * couples:2].set(donor - passed).at[2:2 + 2 * couples:2].set(sink + passed)
    return lengths[jax.random.permutation(jax.random.fold_in(stream_key, 2), number_of)]


def centred(stream_key, shape, deviation, most, cuts=(), held_as=jnp.bfloat16):
    factor_of = shard_levels(stream_key, shape, cuts, -0.22, 0.18) if cuts else 1.0
    values = jax.random.normal(stream_key, shape, jnp.float32) * deviation * factor_of
    return jnp.minimum(jnp.maximum(values, -most), most).astype(held_as)


def setup_inputs(seed: int = 0) -> dict:
    keys = jax.random.split(jax.random.key(seed), 8)
    activations = centred(keys[0], (TOKENS, FF), 1.0, 6.0, ((0, 8), (1, 4)))
    out_grads = centred(keys[1], (TOKENS, D), 1.0, 6.0, ((0, 8),))
    basis_in = centred(keys[2], (FF, FF), FF ** -0.5, 0.03125, ((0, 4), (1, 8)))
    basis_out = centred(keys[3], (D, D), D ** -0.5, 0.0625, ((0, 8), (1, 4)))
    eigenvalues = jnp.clip(jnp.exp(math.log(10.0) - 3.5104718 * jax.random.uniform(keys[4], (D, FF), jnp.float32) ** shard_levels(keys[4], (D, FF), ((0, 4), (1, 8)), -0.2, 0.2)), 0.29882812, 10.0).astype(jnp.bfloat16)
    queries = centred(keys[5], (NQ, D, FF), (D * FF) ** -0.5, 0.00036621094, ((1, 4), (2, 8)))
    doc_ids = jnp.searchsorted(jnp.cumsum(uneven(keys[6], DOCS, TOKENS, DOC_MOST, 2)), jnp.arange(TOKENS), side="right").astype(jnp.int32)
    return dict(activations=activations, out_grads=out_grads, basis_in=basis_in, basis_out=basis_out, eigenvalues=eigenvalues, queries=queries, doc_ids=doc_ids)


DAMPING = 0.1


def reference(activations, out_grads, basis_in, basis_out, eigenvalues, queries, doc_ids):
    rot_acts = jnp.dot(activations, basis_in, preferred_element_type=jnp.float32).astype(jnp.bfloat16)
    rot_grads = jnp.dot(out_grads, basis_out, preferred_element_type=jnp.float32).astype(jnp.bfloat16)
    precond = (queries.astype(jnp.float32) / (eigenvalues.astype(jnp.float32)[None] + DAMPING)).astype(jnp.bfloat16)
    acts_float = rot_acts.astype(jnp.float32)

    def per_query(scaled):
        mixed_rows = jnp.dot(rot_grads, scaled, preferred_element_type=jnp.float32)
        return jnp.sum(mixed_rows * acts_float, axis=1)

    token_scores = lax.map(per_query, precond)
    member = (doc_ids[None, :] == jnp.arange(DOCS, dtype=jnp.int32)[:, None]).astype(jnp.float32)
    return jnp.dot(member, token_scores.T, precision=lax.Precision.HIGHEST)
```

```python
import functools

import jax
import jax.numpy as jnp
from jax import lax
from jax.experimental import pallas as pl
from jax.experimental.pallas import tpu as pltpu
from jax.sharding import PartitionSpec as P

DOC_PER = 2
DAMPING = 0.1
F32 = jnp.float32
BF16 = jnp.bfloat16
ANY = pl.BlockSpec(memory_space=pl.ANY)
VMEM_LIMIT = 67_043_328
PIECES = 8
EARLY = 3


def tile_of(size, most):
    return max(t for t in range(128, most + 1, 128) if size % t == 0)


def grid_of(wide):
    outer = max(o for o in (1, 2, 3, 4) if wide % o == 0)
    return outer, wide // outer


def parts_of(rows_out, narrow):
    return max(p for p in range(1, narrow + 1) if narrow % p == 0 and rows_out % (128 * p) == 0)


def fits(depth, columns, tokens, rows_out, width_out):
    return max(tokens, rows_out) <= depth and width_out + rows_out <= columns


def orders(outer):
    order = []
    for z in range(outer):
        inward = 1 if 2 * z < outer - 1 else -1
        order.append(sorted(range(outer), key=lambda p: (abs(p - z), -inward * (p - z))))
    rank = [[order[z].index(p) for p in range(outer)] for z in range(outer)]
    return order, rank


def lookup(table, i, j):
    value = 0
    for a, row in enumerate(table):
        for b, entry in enumerate(row):
            hit = (i == a) if isinstance(j, int) else jnp.logical_and(i == a, j == b)
            if isinstance(j, int) and b != j:
                continue
            value = value + jnp.where(hit, entry, 0)
    return value


def remote(src, dst, send, recv, device):
    return pltpu.make_async_remote_copy(
        src_ref=src,
        dst_ref=dst,
        send_sem=send,
        recv_sem=recv,
        device_id=device,
        device_id_type=pl.DeviceIdType.MESH,
    )


def greet(wide, narrow):
    w, n = lax.axis_index("wide"), lax.axis_index("narrow")
    barrier = pltpu.get_barrier_semaphore()
    for d in range(1, wide):
        pl.semaphore_signal(
            barrier, inc=1, device_id={"wide": lax.rem(w + d, wide)}, device_id_type=pl.DeviceIdType.MESH
        )
    for d in range(1, narrow):
        pl.semaphore_signal(
            barrier, inc=1, device_id={"narrow": lax.rem(n + d, narrow)}, device_id_type=pl.DeviceIdType.MESH
        )

    def met():
        pl.semaphore_wait(barrier, wide + narrow - 2)

    return met


def score_kernel(
    wide, narrow, docs, acts, grads, basis_in, basis_out, eigenvalues, queries, ids, out,
    pre, basis, acts_all, total, acts_done, core_recv, cross_recv, late_recv,
    rows_spare, weights_spare, grads_own, grads_send, first_recv, second_recv, grads_all, lanes, held, across,
    own_sem, out_sem, eig_sem, query_sem, basis_sem, rows_sem, a2a_s, a2a_r, part_s, part_r,
    up_s, fwd_s, z_r, y_s, y_r, first_s, first_r, second_s, second_r, gz_s, gz_r, gy_s, gy_r,
    core_s, core_r, cross_s, cross_r, late_s, late_r, share_s, share_r, lshare_s, lshare_r,
    send_w, recv_w, send_n, recv_n,
):
    outer, inner = grid_of(wide)
    order, rank = orders(outer)
    cross = narrow // 2
    w, n = lax.axis_index("wide"), lax.axis_index("narrow")
    wo, wi = w // inner, lax.rem(w, inner)
    nx, nc = n // 2, lax.rem(n, 2)
    block, depth_all = acts.shape
    depth, columns = basis.shape[1:]
    chunks = depth_all // depth
    plane = inner * block
    rows_out, width_out = basis_out.shape
    count, width, _ = queries.shape
    slot_plane = [lookup(order, wo, s) for s in range(outer)]

    def side_peer(e):
        return {"wide": wo * inner + lax.rem(wi + e, inner)}

    def line_at(z):
        return {"wide": z * inner + wi}

    def cut(c):
        return pl.ds(pl.multiple_of(c * depth, 128), depth)

    def rows(slot, y):
        return pl.ds(pl.multiple_of(slot * plane + y * block, block), block)

    piece = width // PIECES
    per_slot = depth // piece

    def piece_rows(k, q):
        return pl.ds(pl.multiple_of(q * width + k * piece, 16), piece)

    def eig_rows(k):
        return k // per_slot, pl.ds(pl.multiple_of(lax.rem(k, per_slot) * piece, 16), piece)

    def eig_copy(k):
        slot, at = eig_rows(k)
        return pltpu.make_async_copy(
            eigenvalues.at[pl.ds(pl.multiple_of(k * piece, 16), piece)], basis.at[slot, at], eig_sem.at[k]
        )

    def query_copy(k, q):
        return pltpu.make_async_copy(
            queries.at[q, pl.ds(pl.multiple_of(k * piece, 16), piece)], pre.at[piece_rows(k, q)], query_sem.at[k, q]
        )

    def basis_copy(i):
        slot = lax.rem(i, 3)
        return pltpu.make_async_copy(basis_in.at[cut(lax.rem(i, chunks))], basis.at[slot], basis_sem.at[slot])

    if fits(depth, columns, block * wide, rows_out, width_out):
        weights_out = basis.at[2, pl.ds(0, rows_out), pl.ds(0, width_out)]
        rows_held = basis.at[2, pl.ds(0, block * wide), pl.ds(width_out, rows_out)]
    else:
        weights_out, rows_held = weights_spare, rows_spare
    fetch_out = pltpu.make_async_copy(basis_out, weights_out, out_sem.at[0])

    def own_acts(c):
        return pltpu.make_async_copy(acts.at[:, cut(c)], acts_all.at[rows(0, wi), cut(c)], own_sem.at[c])

    parts = parts_of(rows_out, narrow)
    part, base = lax.rem(n, parts), n // parts * parts
    span = rows_out // parts

    def part_cols(to, p):
        return pl.ds(pl.multiple_of(to * rows_out + p * span, 128), span)

    def held_cols(p):
        return pl.ds(pl.multiple_of(p * span, 128), span)

    def held_rows(source):
        o, i = source // inner, lax.rem(source, inner)
        return pl.ds(pl.multiple_of((i * outer + o) * block, block), block)

    own_rows = pltpu.make_async_copy(
        grads.at[:, part_cols(w, part)], rows_held.at[held_rows(w), held_cols(part)], rows_sem.at[0]
    )

    met = greet(wide, narrow)
    own_rows.start()
    for k in range(EARLY + 1):
        eig_copy(k).start()
        for q in range(count):
            query_copy(k, q).start()
    fetch_out.start()
    for c in range(chunks):
        own_acts(c).start()
    for k in range(EARLY + 1, PIECES):
        eig_copy(k).start()
        for q in range(count):
            query_copy(k, q).start()

    strip = 32

    def precondition(k):
        eig_copy(k).wait()
        for q in range(count):
            query_copy(k, q).wait()
        slot = k // per_slot
        start = lax.rem(k, per_slot) * piece

        def strip_of(r, carry):
            at = pl.ds(pl.multiple_of(start + r * strip, strip), strip)
            scale = 1.0 / (basis[slot, at].astype(F32) + DAMPING)
            for q in range(count):
                here = pl.ds(pl.multiple_of(q * width + k * piece + r * strip, strip), strip)
                pre[here] = (pre[here].astype(F32) * scale).astype(BF16)
            return carry

        lax.fori_loop(0, piece // strip, strip_of, 0)

    for k in range(EARLY):
        precondition(k)
    met()

    def swap(d):
        to = lax.rem(w + d, wide)
        return remote(
            grads.at[:, part_cols(to, part)], rows_held.at[held_rows(w), held_cols(part)],
            a2a_s.at[d], a2a_r.at[d], {"wide": to},
        )

    def part_copy(j):
        return remote(
            rows_held.at[:, held_cols(part)], rows_held.at[:, held_cols(part)],
            part_s.at[j], part_r.at[j], {"narrow": base + lax.rem(part + j, parts)},
        )

    def own_line(c, up):
        to = wo + 1 if up else wo - 1
        slot = lookup(rank, to, wo)
        return remote(
            acts.at[:, cut(c)], acts_all.at[rows(slot, wi), cut(c)], up_s.at[int(up), c], z_r.at[slot, c], line_at(to)
        )

    def line_wait(s, c):
        return remote(
            acts.at[:, cut(c)], acts_all.at[rows(s, wi), cut(c)], fwd_s.at[s, c], z_r.at[s, c], line_at(wo)
        )

    def onward(s):
        above = slot_plane[s] > wo
        to = jnp.where(above, wo - 1, wo + 1)
        return to, jnp.logical_and(to >= 0, to < outer)

    def forward(s, c):
        to, _ = onward(s)
        slot = lookup(rank, to, slot_plane[s])
        return remote(
            acts_all.at[rows(s, wi), cut(c)], acts_all.at[rows(slot, wi), cut(c)],
            fwd_s.at[s, c], z_r.at[slot, c], line_at(to),
        )

    def side_copy(e, s, c):
        source = acts.at[:, cut(c)] if s == 0 else acts_all.at[rows(s, wi), cut(c)]
        return remote(source, acts_all.at[rows(s, wi), cut(c)], y_s.at[e, s, c], y_r.at[e, s, c], side_peer(e))

    def relay(s, c):
        line_wait(s, c).wait_recv()
        _, more = onward(s)

        @pl.when(more)
        def _():
            forward(s, c).start()

        for e in range(1, inner):
            side_copy(e, s, c).start()

    for d in range(1, wide):
        swap(d).start()

    def begin(c, carry):
        for e in range(1, inner):
            side_copy(e, 0, c).start()

        @pl.when(wo + 1 < outer)
        def _():
            own_line(c, True).start()

        @pl.when(wo > 0)
        def _():
            own_line(c, False).start()

        return carry

    lax.fori_loop(0, chunks, begin, 0)

    per_turn = pl.cdiv(PIECES - EARLY, chunks)

    def turn_one(c, carry):
        for j in range(per_turn):
            k = EARLY + c * per_turn + j

            @pl.when(k < PIECES)
            def _():
                precondition(k)

            @pl.when(k == min(per_slot, PIECES) - 1)
            def _():
                basis_copy(0).start()

            @pl.when(k == PIECES - 1)
            def _():
                basis_copy(1).start()

        relay(1, c)

        @pl.when(c == min(1, chunks - 1))
        def _():
            own_rows.wait()
            for d in range(1, wide):
                swap(d).wait_recv()
            for j in range(1, parts):
                part_copy(j).start()

        return carry

    lax.fori_loop(0, chunks, turn_one, 0)

    fetch_out.wait()
    for j in range(1, parts):
        part_copy(j).wait_recv()
    wt = tile_of(width_out, 512)

    def grads_tile(k, carry):
        at = pl.ds(pl.multiple_of(k * wt, 128), wt)
        right = weights_out[:, at]

        def left(i):
            return rows_held[pl.ds(pl.multiple_of(i * outer * block, block), outer * block), :]

        own = jnp.dot(left(wi), right, preferred_element_type=F32)
        grads_own[:, :, at] = own.reshape(outer, block, wt)
        for e in range(1, inner):
            i = lax.rem(wi + e, inner)
            other = jnp.dot(left(i), right, preferred_element_type=F32).astype(BF16)
            grads_send[i, :, :, at] = other.reshape(outer, block, wt)
        return carry

    lax.fori_loop(0, width_out // wt, grads_tile, 0)
    for j in range(1, parts):
        part_copy(j).wait_send()
    basis_copy(2).start()

    def first(e):
        return remote(
            grads_send.at[lax.rem(wi + e, inner)], first_recv.at[e - 1], first_s.at[e], first_r.at[e], side_peer(e)
        )

    def second(d):
        to = lax.rem(wo + d, outer)
        return remote(
            grads_send.at[wi, to], second_recv.at[d - 1], second_s.at[d], second_r.at[d], line_at(to)
        )

    for e in range(1, inner):
        first(e).start()

    pair = 2 * plane
    ct = tile_of(columns, 1792)

    def rotate(g, c):
        i = g * chunks + c
        basis_copy(i).wait()
        slot = lax.rem(i, 3)

        def tile(k, carry):
            at = pl.ds(pl.multiple_of(k * ct, 128), ct)
            value = jnp.dot(
                acts_all[g * pair : (g + 1) * pair, cut(c)], basis[slot, :, at], preferred_element_type=F32
            )

            @pl.when(c == 0)
            def _():
                total[:, at] = value

            @pl.when(c > 0)
            def _():
                total[:, at] += value

            return carry

        lax.fori_loop(0, columns // ct, tile, 0)

        @pl.when(i + 3 < 2 * chunks)
        def _():
            basis_copy(i + 3).start()

    def turn_two(c, carry):
        own_acts(c).wait()
        for e in range(1, inner):
            side_copy(e, 0, c).wait_recv()
        relay(2, c)
        for e in range(1, inner):
            side_copy(e, 1, c).wait_recv()
        rotate(0, c)
        return carry

    lax.fori_loop(0, chunks, turn_two, 0)

    partner = {"narrow": nx * 2 + (1 - nc)}
    mine = pl.ds(pl.multiple_of(nc * plane, plane), plane)
    theirs = pl.ds(pl.multiple_of((1 - nc) * plane, plane), plane)
    cols = 4 if columns % 512 == 0 else 1
    cw = columns // cols

    def lane(k):
        return pl.ds(pl.multiple_of(k * cw, 128), cw)

    def cross_peer(d):
        return {"narrow": lax.rem(nx + d, cross) * 2 + nc}

    def core_copy(g):
        return remote(total.at[theirs], core_recv, core_s.at[g], core_r.at[g], partner)

    def cross_copy(d):
        return remote(total.at[mine], cross_recv.at[d - 1], cross_s.at[d], cross_r.at[d], cross_peer(d))

    def done_rows(g):
        return pl.ds(pl.multiple_of((2 * g + nc) * plane, plane), plane)

    def share_copy():
        return remote(
            acts_done.at[done_rows(0)], acts_done.at[done_rows(0)], share_s.at[0], share_r.at[0], partner
        )

    def late_copy(d, k):
        return remote(
            acts_done.at[done_rows(1), lane(k)], late_recv.at[d - 1, :, lane(k)], late_s.at[d, k], late_r.at[d, k], cross_peer(d)
        )

    def late_share(k):
        here = acts_done.at[done_rows(1), lane(k)]
        return remote(here, here, lshare_s.at[k], lshare_r.at[k], partner)

    core_copy(0).start()
    core_copy(0).wait_recv()

    def core_sum(k, carry):
        total[mine, lane(k)] += core_recv[:, lane(k)]
        return carry

    lax.fori_loop(0, cols, core_sum, 0)
    for d in range(1, cross):
        cross_copy(d).start()

    def turn_three(c, carry):
        relay(3, c)
        return carry

    lax.fori_loop(0, chunks, turn_three, 0)

    for e in range(1, inner):
        first(e).wait_recv()
    for o in range(outer):
        value = grads_own[o]
        for e in range(1, inner):
            value = value + first_recv[e - 1, o].astype(F32)
        grads_own[o] = value
        grads_send[wi, o] = value.astype(BF16)
    for d in range(1, outer):
        second(d).start()

    def group_done():
        for d in range(1, cross):
            cross_copy(d).wait_recv()

        def cross_sum(k, carry):
            value = total[mine, lane(k)]
            for d in range(1, cross):
                value = value + cross_recv[d - 1, :, lane(k)]
            acts_done[done_rows(0), lane(k)] = value.astype(BF16)
            return carry

        lax.fori_loop(0, cols, cross_sum, 0)
        share_copy().start()

    for d in range(1, outer):
        second(d).wait_recv()
    value = grads_own[wo]
    for d in range(1, outer):
        value = value + second_recv[d - 1].astype(F32)
    grads_all[0, wi] = value.astype(BF16)

    def gline(d):
        to = lax.rem(wo + d, outer)
        slot = lookup(rank, to, wo)
        return remote(grads_all.at[0, wi], grads_all.at[slot, wi], gz_s.at[d], gz_r.at[slot], line_at(to))

    def gline_wait(s):
        return remote(grads_all.at[0, wi], grads_all.at[s, wi], gz_s.at[s], gz_r.at[s], line_at(wo))

    def gside(e, s):
        return remote(
            grads_all.at[s, wi], grads_all.at[s, wi], gy_s.at[e, s], gy_r.at[e, s], side_peer(e)
        )

    for d in range(1, outer):
        gline(d).start()
    for e in range(1, inner):
        gside(e, 0).start()

    group_done()
    core_copy(0).wait_send()
    for d in range(1, cross):
        cross_copy(d).wait_send()

    def turn_four(c, carry):
        for s in (2, 3):
            for e in range(1, inner):
                side_copy(e, s, c).wait_recv()
        rotate(1, c)
        return carry

    lax.fori_loop(0, chunks, turn_four, 0)
    share_copy().wait_recv()
    core_copy(1).start()
    for s in range(1, outer):
        gline_wait(s).wait_recv()
        for e in range(1, inner):
            gside(e, s).start()
    core_copy(1).wait_recv()

    def late_sum(k, carry):
        value = total[mine, lane(k)] + core_recv[:, lane(k)]
        total[mine, lane(k)] = value
        acts_done[done_rows(1), lane(k)] = value.astype(BF16)
        for d in range(1, cross):
            late_copy(d, k).start()
        return carry

    lax.fori_loop(0, cols, late_sum, 0)

    lanes[...] = jnp.zeros_like(lanes)

    def mix(g, k):
        left = grads_all[2 * g : 2 * g + 2].reshape(pair, width)
        here = slice(g * pair, (g + 1) * pair)
        for q in range(count):
            mixed = jnp.dot(left, pre[q * width : (q + 1) * width, lane(k)], preferred_element_type=F32)
            right = acts_done[here, lane(k)].astype(F32)
            value = lanes[q, here]
            for j in range(cw // 128):
                value = value + mixed[:, j * 128 : (j + 1) * 128] * right[:, j * 128 : (j + 1) * 128]
            lanes[q, here] = value

    for e in range(1, inner):
        for s in (0, 1):
            gside(e, s).wait_recv()

    def mix_early(k, carry):
        mix(0, k)
        return carry

    lax.fori_loop(0, cols, mix_early, 0)
    for e in range(1, inner):
        for s in (2, 3):
            gside(e, s).wait_recv()

    def late_done(k):
        for d in range(1, cross):
            late_copy(d, k).wait()
        value = total[mine, lane(k)]
        for d in range(1, cross):
            value = value + late_recv[d - 1, :, lane(k)].astype(F32)
        acts_done[done_rows(1), lane(k)] = value.astype(BF16)
        late_share(k).start()

    late_done(0)

    def mix_late(k, carry):
        @pl.when(k + 1 < cols)
        def _():
            late_done(k + 1)

        late_share(k).wait_recv()
        mix(1, k)
        return carry

    lax.fori_loop(0, cols, mix_late, 0)

    _, rows_pad, docs_pad = across.shape
    row = lax.broadcasted_iota(jnp.int32, (rows_pad, docs_pad), 0)
    value = jnp.zeros((rows_pad, docs_pad), F32)
    members = [
        (ids[slot_plane[s]] == lax.broadcasted_iota(jnp.int32, (docs_pad, plane), 0)).astype(F32)
        for s in range(outer)
    ]
    for q in range(count):
        doc_lanes = jnp.zeros((docs_pad, 128), F32)
        for s in range(outer):
            doc_lanes = doc_lanes + jnp.dot(
                members[s],
                lanes[q, s * plane : (s + 1) * plane],
                precision=lax.Precision.HIGHEST,
                preferred_element_type=F32,
            )
        value = jnp.where(row == q, jnp.sum(doc_lanes, axis=1)[None, :], value)
    across[n] = value

    def over_narrow(d):
        return remote(across.at[n], across.at[n], send_n.at[d], recv_n.at[d], {"narrow": lax.rem(n + d, narrow)})

    def over_wide(d):
        return remote(held.at[w], held.at[w], send_w.at[d], recv_w.at[d], {"wide": lax.rem(w + d, wide)})

    for d in range(1, narrow):
        over_narrow(d).start()
    for d in range(1, narrow):
        over_narrow(d).wait_recv()
    value = across[0]
    for d in range(1, narrow):
        value = value + across[d]
    held[w] = value
    for d in range(1, wide):
        over_wide(d).start()
    for d in range(1, wide):
        over_wide(d).wait_recv()
    value = held[0]
    for d in range(1, wide):
        value = value + held[d]
    out[...] = value[: out.shape[0], : out.shape[1]]

    for d in range(1, wide):
        swap(d).wait_send()

    def drain(c, carry):
        @pl.when(wo + 1 < outer)
        def _():
            own_line(c, True).wait_send()

        @pl.when(wo > 0)
        def _():
            own_line(c, False).wait_send()

        for s in range(1, outer):
            _, more = onward(s)

            @pl.when(more)
            def _():
                forward(s, c).wait_send()

        for s in range(outer):
            for e in range(1, inner):
                side_copy(e, s, c).wait_send()
        return carry

    lax.fori_loop(0, chunks, drain, 0)
    for e in range(1, inner):
        first(e).wait_send()
        for s in range(outer):
            gside(e, s).wait_send()
    for d in range(1, outer):
        second(d).wait_send()
        gline(d).wait_send()
    core_copy(1).wait_send()
    share_copy().wait_send()
    for k in range(cols):
        late_share(k).wait_send()
    for d in range(1, narrow):
        over_narrow(d).wait_send()
    for d in range(1, wide):
        over_wide(d).wait_send()


def score(wide, narrow, activations, out_grads, basis_in, basis_out, eigenvalues, queries, doc_ids):
    outer, inner = grid_of(wide)
    cross = narrow // 2
    block, depth_all = activations.shape
    tokens = block * wide
    plane = block * inner
    docs = DOC_PER * wide
    depth = tile_of(depth_all, 1024)
    chunks = depth_all // depth
    columns = basis_in.shape[1]
    rows_out, width_out = basis_out.shape
    count, width, _ = queries.shape
    cols = 4 if columns % 512 == 0 else 1
    parts = parts_of(rows_out, narrow)
    inside = fits(depth, columns, tokens, rows_out, width_out)
    rows_pad, docs_pad = pl.cdiv(count, 8) * 8, pl.cdiv(docs, 128) * 128
    dma = pltpu.SemaphoreType.DMA
    scores = pl.pallas_call(
        functools.partial(score_kernel, wide, narrow, docs),
        out_shape=jax.ShapeDtypeStruct((count, docs), F32),
        in_specs=[ANY] * 6 + [pl.BlockSpec(memory_space=pltpu.VMEM)],
        out_specs=pl.BlockSpec(memory_space=pltpu.VMEM),
        scratch_shapes=[
            pltpu.VMEM((count * width, columns), BF16),
            pltpu.VMEM((3, depth, columns), BF16),
            pltpu.VMEM((tokens, depth_all), BF16),
            pltpu.VMEM((2 * plane, columns), F32),
            pltpu.VMEM((tokens, columns), BF16),
            pltpu.VMEM((plane, columns), F32),
            pltpu.VMEM((cross - 1, plane, columns), F32),
            pltpu.VMEM((cross - 1, plane, columns), BF16),
            pltpu.VMEM((16, 128) if inside else (tokens, rows_out), BF16),
            pltpu.VMEM((16, 128) if inside else (rows_out, width_out), BF16),
            pltpu.VMEM((outer, block, width_out), F32),
            pltpu.VMEM((inner, outer, block, width_out), BF16),
            pltpu.VMEM((inner - 1, outer, block, width_out), BF16),
            pltpu.VMEM((outer - 1, block, width_out), BF16),
            pltpu.VMEM((outer, inner, block, width_out), BF16),
            pltpu.VMEM((count, tokens, 128), F32),
            pltpu.VMEM((wide, rows_pad, docs_pad), F32),
            pltpu.VMEM((narrow, rows_pad, docs_pad), F32),
            dma((chunks,)),
            dma((1,)),
            dma((PIECES,)),
            dma((PIECES, count)),
            dma((3,)),
            dma((1,)),
            dma((wide,)),
            dma((wide,)),
            dma((parts,)),
            dma((parts,)),
            dma((2, chunks)),
            dma((outer, chunks)),
            dma((outer, chunks)),
            dma((inner, outer, chunks)),
            dma((inner, outer, chunks)),
            dma((inner,)),
            dma((inner,)),
            dma((outer,)),
            dma((outer,)),
            dma((outer,)),
            dma((outer,)),
            dma((inner, outer)),
            dma((inner, outer)),
            dma((2,)),
            dma((2,)),
            dma((cross,)),
            dma((cross,)),
            dma((cross, cols)),
            dma((cross, cols)),
            dma((1,)),
            dma((1,)),
            dma((cols,)),
            dma((cols,)),
            dma((wide,)),
            dma((wide,)),
            dma((narrow,)),
            dma((narrow,)),
        ],
        compiler_params=pltpu.CompilerParams(
            collective_id=0, has_side_effects=True, vmem_limit_bytes=VMEM_LIMIT
        ),
        name="score",
    )(activations, out_grads, basis_in, basis_out, eigenvalues, queries, doc_ids.reshape(outer, 1, plane))
    return scores.T


def solution(mesh):
    wide, narrow = mesh.shape["wide"], mesh.shape["narrow"]

    def shards(activations, out_grads, basis_in, basis_out, eigenvalues, queries, doc_ids):
        return score(
            wide, narrow, activations, out_grads, basis_in, basis_out, eigenvalues, queries, doc_ids
        )

    return jax.shard_map(
        shards,
        mesh=mesh,
        in_specs=(
            P("wide", "narrow"),
            P("wide", None),
            P("narrow", "wide"),
            P("wide", "narrow"),
            P("narrow", "wide"),
            P(None, "narrow", "wide"),
            P(),
        ),
        out_specs=P(),
        check_vma=False,
    )
```

```python
import functools

import jax
import jax.numpy as jnp
from jax import lax
from jax.experimental import pallas as pl
from jax.experimental.pallas import tpu as pltpu
from jax.sharding import PartitionSpec as P

DOC_PER = 2
DAMPING = 0.1
F32 = jnp.float32
BF16 = jnp.bfloat16
ANY = pl.BlockSpec(memory_space=pl.ANY)
VMEM_LIMIT = 67_043_328
PIECES = 16
EARLY = 2
AHEAD = 4


def tile_of(size, most):
    return max(t for t in range(128, most + 1, 128) if size % t == 0)


def grid_of(wide):
    outer = max(o for o in (1, 2, 3, 4) if wide % o == 0)
    return outer, wide // outer


def parts_of(rows_out, narrow):
    return max(p for p in range(1, narrow + 1) if narrow % p == 0 and rows_out % (128 * p) == 0)


def fits(depth, columns, tokens, rows_out, width_out):
    return max(tokens, rows_out) <= depth and width_out + rows_out <= columns


def orders(outer):
    order = []
    for z in range(outer):
        inward = 1 if 2 * z < outer - 1 else -1
        order.append(sorted(range(outer), key=lambda p: (abs(p - z), -inward * (p - z))))
    rank = [[order[z].index(p) for p in range(outer)] for z in range(outer)]
    return order, rank


def lookup(table, i, j):
    value = 0
    for a, row in enumerate(table):
        for b, entry in enumerate(row):
            hit = (i == a) if isinstance(j, int) else jnp.logical_and(i == a, j == b)
            if isinstance(j, int) and b != j:
                continue
            value = value + jnp.where(hit, entry, 0)
    return value


def remote(src, dst, send, recv, device):
    return pltpu.make_async_remote_copy(
        src_ref=src,
        dst_ref=dst,
        send_sem=send,
        recv_sem=recv,
        device_id=device,
        device_id_type=pl.DeviceIdType.MESH,
    )


def greet(wide, narrow):
    w, n = lax.axis_index("wide"), lax.axis_index("narrow")
    barrier = pltpu.get_barrier_semaphore()
    for d in range(1, wide):
        pl.semaphore_signal(
            barrier, inc=1, device_id={"wide": lax.rem(w + d, wide)}, device_id_type=pl.DeviceIdType.MESH
        )
    for d in range(1, narrow):
        pl.semaphore_signal(
            barrier, inc=1, device_id={"narrow": lax.rem(n + d, narrow)}, device_id_type=pl.DeviceIdType.MESH
        )

    def met():
        pl.semaphore_wait(barrier, wide + narrow - 2)

    return met


def score_kernel(
    wide, narrow, docs, acts, grads, basis_in, basis_out, eigenvalues, queries, ids, out,
    pre, basis, acts_all, total, acts_done, core_recv, cross_recv, late_recv,
    rows_spare, weights_spare, grads_own, grads_send, first_recv, second_recv, grads_all, lanes, held, across,
    own_sem, out_sem, eig_sem, query_sem, basis_sem, rows_sem, a2a_s, a2a_r, part_s, part_r,
    up_s, fwd_s, z_r, y_s, y_r, first_s, first_r, second_s, second_r, gz_s, gz_r, gy_s, gy_r,
    core_s, core_r, cross_s, cross_r, late_s, late_r, share_s, share_r, lshare_s, lshare_r,
    send_w, recv_w, send_n, recv_n,
):
    outer, inner = grid_of(wide)
    order, rank = orders(outer)
    cross = narrow // 2
    w, n = lax.axis_index("wide"), lax.axis_index("narrow")
    wo, wi = w // inner, lax.rem(w, inner)
    nx, nc = n // 2, lax.rem(n, 2)
    block, depth_all = acts.shape
    depth, columns = basis.shape[1:]
    chunks = depth_all // depth
    plane = inner * block
    rows_out, width_out = basis_out.shape
    count, width, _ = queries.shape
    slot_plane = [lookup(order, wo, s) for s in range(outer)]

    def side_peer(e):
        return {"wide": wo * inner + lax.rem(wi + e, inner)}

    def line_at(z):
        return {"wide": z * inner + wi}

    def cut(c):
        return pl.ds(pl.multiple_of(c * depth, 128), depth)

    def rows(slot, y):
        return pl.ds(pl.multiple_of(slot * plane + y * block, block), block)

    piece = width // PIECES
    per_slot = depth // piece

    def piece_rows(k, q):
        return pl.ds(pl.multiple_of(q * width + k * piece, 16), piece)

    def eig_rows(k):
        return k // per_slot, pl.ds(pl.multiple_of(lax.rem(k, per_slot) * piece, 16), piece)

    def eig_copy(k):
        slot, at = eig_rows(k)
        return pltpu.make_async_copy(
            eigenvalues.at[pl.ds(pl.multiple_of(k * piece, 16), piece)], basis.at[slot, at], eig_sem.at[lax.rem(k, AHEAD)]
        )

    def query_copy(k, q):
        return pltpu.make_async_copy(
            queries.at[q, pl.ds(pl.multiple_of(k * piece, 16), piece)],
            pre.at[piece_rows(k, q)],
            query_sem.at[lax.rem(k, AHEAD), q],
        )

    def basis_copy(i):
        slot = lax.rem(i, 3)
        return pltpu.make_async_copy(basis_in.at[cut(lax.rem(i, chunks))], basis.at[slot], basis_sem.at[slot])

    if fits(depth, columns, block * wide, rows_out, width_out):
        weights_out = basis.at[2, pl.ds(0, rows_out), pl.ds(0, width_out)]
        rows_held = basis.at[2, pl.ds(0, block * wide), pl.ds(width_out, rows_out)]
    else:
        weights_out, rows_held = weights_spare, rows_spare
    fetch_out = pltpu.make_async_copy(basis_out, weights_out, out_sem.at[0])

    own_acts = pltpu.make_async_copy(acts, acts_all.at[rows(0, wi)], own_sem.at[0])

    parts = parts_of(rows_out, narrow)
    part, base = lax.rem(n, parts), n // parts * parts
    span = rows_out // parts

    def part_cols(to, p):
        return pl.ds(pl.multiple_of(to * rows_out + p * span, 128), span)

    def held_cols(p):
        return pl.ds(pl.multiple_of(p * span, 128), span)

    def held_rows(source):
        o, i = source // inner, lax.rem(source, inner)
        return pl.ds(pl.multiple_of((i * outer + o) * block, block), block)

    own_rows = pltpu.make_async_copy(
        grads.at[:, part_cols(w, part)], rows_held.at[held_rows(w), held_cols(part)], rows_sem.at[0]
    )

    met = greet(wide, narrow)
    own_rows.start()

    def fetch_piece(k):
        eig_copy(k).start()
        for q in range(count):
            query_copy(k, q).start()

    for k in range(AHEAD - 1):
        fetch_piece(k)

    strip = 32

    def precondition(k):
        @pl.when(k + AHEAD - 1 < PIECES)
        def _():
            fetch_piece(k + AHEAD - 1)

        eig_copy(k).wait()
        for q in range(count):
            query_copy(k, q).wait()
        slot = k // per_slot
        start = lax.rem(k, per_slot) * piece

        def strip_of(r, carry):
            at = pl.ds(pl.multiple_of(start + r * strip, strip), strip)
            scale = 1.0 / (basis[slot, at].astype(F32) + DAMPING)
            for q in range(count):
                here = pl.ds(pl.multiple_of(q * width + k * piece + r * strip, strip), strip)
                pre[here] = (pre[here].astype(F32) * scale).astype(BF16)
            return carry

        lax.fori_loop(0, piece // strip, strip_of, 0)

    for k in range(EARLY):
        precondition(k)
    met()

    def swap(d):
        to = lax.rem(w + d, wide)
        return remote(
            grads.at[:, part_cols(to, part)], rows_held.at[held_rows(w), held_cols(part)],
            a2a_s.at[0], a2a_r.at[d], {"wide": to},
        )

    def part_copy(j):
        return remote(
            rows_held.at[:, held_cols(part)], rows_held.at[:, held_cols(part)],
            part_s.at[j], part_r.at[j], {"narrow": base + lax.rem(part + j, parts)},
        )

    def own_line(c, up):
        to = wo + 1 if up else wo - 1
        slot = lookup(rank, to, wo)
        return remote(
            acts.at[:, cut(c)], acts_all.at[rows(slot, wi), cut(c)], up_s.at[int(up)], z_r.at[slot, c], line_at(to)
        )

    def line_wait(s, c):
        return remote(
            acts.at[:, cut(c)], acts_all.at[rows(s, wi), cut(c)], fwd_s.at[s], z_r.at[s, c], line_at(wo)
        )

    def onward(s):
        above = slot_plane[s] > wo
        to = jnp.where(above, wo - 1, wo + 1)
        return to, jnp.logical_and(to >= 0, to < outer)

    def forward(s, c):
        to, _ = onward(s)
        slot = lookup(rank, to, slot_plane[s])
        return remote(
            acts_all.at[rows(s, wi), cut(c)], acts_all.at[rows(slot, wi), cut(c)],
            fwd_s.at[s], z_r.at[slot, c], line_at(to),
        )

    def side_copy(e, s, c):
        source = acts.at[:, cut(c)] if s == 0 else acts_all.at[rows(s, wi), cut(c)]
        return remote(source, acts_all.at[rows(s, wi), cut(c)], y_s.at[e - 1, s], y_r.at[e - 1, s, c], side_peer(e))

    amid = jnp.logical_and(wo > 0, wo < outer - 1)

    def arrive(s, c):
        line_wait(s, c).wait_recv()
        _, more = onward(s)

        @pl.when(more)
        def _():
            forward(s, c).start()

    def across_side(s, c):
        for e in range(1, inner):
            side_copy(e, s, c).start()

    for d in range(1, wide):
        swap(d).start()

    def begin(c, carry):
        for e in range(1, inner):
            side_copy(e, 0, c).start()

        @pl.when(wo + 1 < outer)
        def _():
            own_line(c, True).start()

        @pl.when(wo > 0)
        def _():
            own_line(c, False).start()

        return carry

    lax.fori_loop(0, chunks, begin, 0)

    per_turn = pl.cdiv(PIECES - EARLY, chunks)

    def turn_one(c, carry):
        for j in range(per_turn):
            k = EARLY + c * per_turn + j

            @pl.when(k < PIECES)
            def _():
                precondition(k)

            @pl.when(k == min(per_slot, PIECES) - 1)
            def _():
                basis_copy(0).start()

            @pl.when(k == PIECES - 1)
            def _():
                basis_copy(1).start()

        arrive(1, c)
        across_side(1, c)

        @pl.when(amid)
        def _():
            arrive(2, c)

        @pl.when(c == 0)
        def _():
            fetch_out.start()
            own_acts.start()

        @pl.when(c == min(1, chunks - 1))
        def _():
            own_rows.wait()
            for d in range(1, wide):
                swap(d).wait_recv()
            for j in range(1, parts):
                part_copy(j).start()

        return carry

    lax.fori_loop(0, chunks, turn_one, 0)

    fetch_out.wait()
    for j in range(1, parts):
        part_copy(j).wait_recv()
    wt = tile_of(width_out, 512)

    def grads_tile(k, carry):
        at = pl.ds(pl.multiple_of(k * wt, 128), wt)
        right = weights_out[:, at]

        def left(i):
            return rows_held[pl.ds(pl.multiple_of(i * outer * block, block), outer * block), :]

        own = jnp.dot(left(wi), right, preferred_element_type=F32)
        grads_own[:, :, at] = own.reshape(outer, block, wt)
        for e in range(1, inner):
            i = lax.rem(wi + e, inner)
            other = jnp.dot(left(i), right, preferred_element_type=F32).astype(BF16)
            grads_send[i, :, :, at] = other.reshape(outer, block, wt)
        return carry

    lax.fori_loop(0, width_out // wt, grads_tile, 0)
    for j in range(1, parts):
        part_copy(j).wait_send()
    basis_copy(2).start()

    def first(e):
        return remote(
            grads_send.at[lax.rem(wi + e, inner)], first_recv.at[e - 1], first_s.at[e], first_r.at[e], side_peer(e)
        )

    def second(d):
        to = lax.rem(wo + d, outer)
        return remote(
            grads_send.at[wi, to], second_recv.at[d - 1], second_s.at[d], second_r.at[d], line_at(to)
        )

    for e in range(1, inner):
        first(e).start()

    pair = 2 * plane
    ct = tile_of(columns, 1792)

    def rotate(g, c):
        i = g * chunks + c
        basis_copy(i).wait()
        slot = lax.rem(i, 3)

        def tile(k, carry):
            at = pl.ds(pl.multiple_of(k * ct, 128), ct)
            value = jnp.dot(
                acts_all[g * pair : (g + 1) * pair, cut(c)], basis[slot, :, at], preferred_element_type=F32
            )

            @pl.when(c == 0)
            def _():
                total[:, at] = value

            @pl.when(c > 0)
            def _():
                total[:, at] += value

            return carry

        lax.fori_loop(0, columns // ct, tile, 0)

        @pl.when(i + 3 < 2 * chunks)
        def _():
            basis_copy(i + 3).start()

    def turn_two(c, carry):
        @pl.when(jnp.logical_not(amid))
        def _():
            arrive(2, c)

        across_side(2, c)

        @pl.when(amid)
        def _():
            arrive(3, c)

        for e in range(1, inner):
            side_copy(e, 0, c).wait_recv()
        for e in range(1, inner):
            side_copy(e, 1, c).wait_recv()
        rotate(0, c)
        return carry

    own_acts.wait()
    lax.fori_loop(0, chunks, turn_two, 0)

    partner = {"narrow": nx * 2 + (1 - nc)}
    mine = pl.ds(pl.multiple_of(nc * plane, plane), plane)
    theirs = pl.ds(pl.multiple_of((1 - nc) * plane, plane), plane)
    cols = 7 if columns % 896 == 0 else 1
    cw = columns // cols

    def lane(k):
        return pl.ds(pl.multiple_of(k * cw, 128), cw)

    def cross_peer(d):
        return {"narrow": lax.rem(nx + d, cross) * 2 + nc}

    def core_copy(g):
        return remote(total.at[theirs], core_recv, core_s.at[g], core_r.at[g], partner)

    def cross_copy(d):
        return remote(core_recv, cross_recv.at[d - 1], cross_s.at[d], cross_r.at[d], cross_peer(d))

    def done_rows(g):
        return pl.ds(pl.multiple_of((2 * g + nc) * plane, plane), plane)

    def share_copy():
        return remote(
            acts_done.at[done_rows(0)], acts_done.at[done_rows(0)], share_s.at[0], share_r.at[0], partner
        )

    def late_copy(d, k):
        return remote(
            acts_done.at[done_rows(1), lane(k)], late_recv.at[d - 1, :, lane(k)], late_s.at[d, k], late_r.at[d, k], cross_peer(d)
        )

    def late_share(k):
        here = acts_done.at[done_rows(1), lane(k)]
        return remote(here, here, lshare_s.at[k], lshare_r.at[k], partner)

    core_copy(0).start()
    core_copy(0).wait_recv()

    def core_sum(k, carry):
        core_recv[:, lane(k)] += total[mine, lane(k)]
        return carry

    lax.fori_loop(0, cols, core_sum, 0)
    for d in range(1, cross):
        cross_copy(d).start()

    def turn_three(c, carry):
        @pl.when(jnp.logical_not(amid))
        def _():
            arrive(3, c)

        across_side(3, c)
        return carry

    lax.fori_loop(0, chunks, turn_three, 0)

    for e in range(1, inner):
        first(e).wait_recv()
    for o in range(outer):
        value = grads_own[o]
        for e in range(1, inner):
            value = value + first_recv[e - 1, o].astype(F32)
        grads_own[o] = value
        grads_send[wi, o] = value.astype(BF16)
    for d in range(1, outer):
        second(d).start()

    def group_done():
        for d in range(1, cross):
            cross_copy(d).wait()

        def cross_sum(k, carry):
            value = core_recv[:, lane(k)]
            for d in range(1, cross):
                value = value + cross_recv[d - 1, :, lane(k)]
            acts_done[done_rows(0), lane(k)] = value.astype(BF16)
            return carry

        lax.fori_loop(0, cols, cross_sum, 0)
        share_copy().start()

    def gline(d):
        to = lax.rem(wo + d, outer)
        slot = lookup(rank, to, wo)
        return remote(grads_all.at[0, wi], grads_all.at[slot, wi], gz_s.at[d], gz_r.at[slot], line_at(to))

    def gline_wait(s):
        return remote(grads_all.at[0, wi], grads_all.at[s, wi], gz_s.at[s], gz_r.at[s], line_at(wo))

    def gside(e, s):
        return remote(
            grads_all.at[s, wi], grads_all.at[s, wi], gy_s.at[e, s], gy_r.at[e, s], side_peer(e)
        )

    core_copy(0).wait_send()

    def turn_four(c, carry):
        for s in (2, 3):
            for e in range(1, inner):
                side_copy(e, s, c).wait_recv()
        rotate(1, c)

        @pl.when(c == chunks // 2)
        def _():
            for d in range(1, outer):
                second(d).wait_recv()
            value = grads_own[wo]
            for d in range(1, outer):
                value = value + second_recv[d - 1].astype(F32)
            grads_all[0, wi] = value.astype(BF16)

            for d in range(1, outer):
                gline(d).start()
            for e in range(1, inner):
                gside(e, 0).start()

        @pl.when(c == chunks - 2)
        def _():
            group_done()

        return carry

    lax.fori_loop(0, chunks, turn_four, 0)
    share_copy().wait_recv()
    core_copy(1).start()

    def grads_across(s):
        gline_wait(s).wait_recv()
        for e in range(1, inner):
            gside(e, s).start()

    grads_across(1)
    core_copy(1).wait_recv()

    def late_sum(k, carry):
        value = total[mine, lane(k)] + core_recv[:, lane(k)]
        total[mine, lane(k)] = value
        acts_done[done_rows(1), lane(k)] = value.astype(BF16)
        for d in range(1, cross):
            late_copy(d, k).start()
        return carry

    lax.fori_loop(0, cols, late_sum, 0)
    for s in range(2, outer):
        grads_across(s)

    lanes[...] = jnp.zeros_like(lanes)

    def mix(g, k):
        left = grads_all[2 * g : 2 * g + 2].reshape(pair, width)
        here = slice(g * pair, (g + 1) * pair)
        for q in range(count):
            mixed = jnp.dot(left, pre[q * width : (q + 1) * width, lane(k)], preferred_element_type=F32)
            right = acts_done[here, lane(k)].astype(F32)
            value = jnp.zeros((pair, 128), F32)
            for j in range(cw // 128):
                value = value + mixed[:, j * 128 : (j + 1) * 128] * right[:, j * 128 : (j + 1) * 128]
            for h in range(2):
                there = pl.ds(pl.multiple_of(slot_plane[2 * g + h] * plane, plane), plane)
                lanes[q, there] += value[h * plane : (h + 1) * plane]

    for e in range(1, inner):
        for s in (0, 1):
            gside(e, s).wait_recv()

    def mix_early(k, carry):
        mix(0, k)
        return carry

    lax.fori_loop(0, cols, mix_early, 0)
    for e in range(1, inner):
        for s in (2, 3):
            gside(e, s).wait_recv()

    def late_done(k):
        for d in range(1, cross):
            late_copy(d, k).wait()
        value = total[mine, lane(k)]
        for d in range(1, cross):
            value = value + late_recv[d - 1, :, lane(k)].astype(F32)
        acts_done[done_rows(1), lane(k)] = value.astype(BF16)
        late_share(k).start()

    late_done(0)

    def mix_late(k, carry):
        @pl.when(k + 1 < cols)
        def _():
            late_done(k + 1)

        late_share(k).wait_recv()
        mix(1, k)
        return carry

    lax.fori_loop(0, cols, mix_late, 0)

    _, rows_pad, docs_pad = across.shape
    row = lax.broadcasted_iota(jnp.int32, (rows_pad, docs_pad), 0)
    value = jnp.zeros((rows_pad, docs_pad), F32)
    tokens = block * wide
    named = jnp.broadcast_to(ids[...].reshape(1, tokens), (docs_pad, tokens))
    member = (named == lax.broadcasted_iota(jnp.int32, (docs_pad, tokens), 0)).astype(F32)
    for q in range(count):
        doc_lanes = jnp.dot(member, lanes[q], precision=lax.Precision.HIGHEST, preferred_element_type=F32)
        value = jnp.where(row == q, jnp.sum(doc_lanes, axis=1)[None, :], value)
    across[n] = value

    def over_narrow(d):
        return remote(across.at[n], across.at[n], send_n.at[0], recv_n.at[d], {"narrow": lax.rem(n + d, narrow)})

    def over_wide(d):
        return remote(held.at[w], held.at[w], send_w.at[0], recv_w.at[d], {"wide": lax.rem(w + d, wide)})

    for d in range(1, narrow):
        over_narrow(d).start()
    for d in range(1, narrow):
        over_narrow(d).wait_recv()
    value = across[0]
    for d in range(1, narrow):
        value = value + across[d]
    held[w] = value
    for d in range(1, wide):
        over_wide(d).start()
    for d in range(1, wide):
        over_wide(d).wait_recv()
    value = held[0]
    for d in range(1, wide):
        value = value + held[d]
    out[...] = value[: out.shape[0], : out.shape[1]]

    def left(source, sem):
        pltpu.make_async_copy(source, source, sem).wait()

    left(rows_held.at[pl.ds(0, (wide - 1) * block), held_cols(0)], a2a_s.at[0])
    row_block = acts_all.at[rows(0, wi)]

    @pl.when(wo + 1 < outer)
    def _():
        left(row_block, up_s.at[1])

    @pl.when(wo > 0)
    def _():
        left(row_block, up_s.at[0])

    for s in range(1, outer):
        _, more = onward(s)

        @pl.when(more)
        def _():
            left(row_block, fwd_s.at[s])

    for s in range(outer):
        for e in range(1, inner):
            left(row_block, y_s.at[e - 1, s])
    for e in range(1, inner):
        first(e).wait_send()
        for s in range(outer):
            gside(e, s).wait_send()
    for d in range(1, outer):
        second(d).wait_send()
        gline(d).wait_send()
    core_copy(1).wait_send()
    share_copy().wait_send()
    for k in range(cols):
        late_share(k).wait_send()
    left(across.at[pl.ds(0, narrow - 1)], send_n.at[0])
    left(held.at[pl.ds(0, wide - 1)], send_w.at[0])


def score(wide, narrow, activations, out_grads, basis_in, basis_out, eigenvalues, queries, doc_ids):
    outer, inner = grid_of(wide)
    cross = narrow // 2
    block, depth_all = activations.shape
    tokens = block * wide
    plane = block * inner
    docs = DOC_PER * wide
    depth = tile_of(depth_all, 1024)
    chunks = depth_all // depth
    columns = basis_in.shape[1]
    rows_out, width_out = basis_out.shape
    count, width, _ = queries.shape
    cols = 7 if columns % 896 == 0 else 1
    parts = parts_of(rows_out, narrow)
    inside = fits(depth, columns, tokens, rows_out, width_out)
    rows_pad, docs_pad = pl.cdiv(count, 8) * 8, pl.cdiv(docs, 128) * 128
    dma = pltpu.SemaphoreType.DMA
    scores = pl.pallas_call(
        functools.partial(score_kernel, wide, narrow, docs),
        out_shape=jax.ShapeDtypeStruct((count, docs), F32),
        in_specs=[ANY] * 6 + [pl.BlockSpec(memory_space=pltpu.VMEM)],
        out_specs=pl.BlockSpec(memory_space=pltpu.VMEM),
        scratch_shapes=[
            pltpu.VMEM((count * width, columns), BF16),
            pltpu.VMEM((3, depth, columns), BF16),
            pltpu.VMEM((tokens, depth_all), BF16),
            pltpu.VMEM((2 * plane, columns), F32),
            pltpu.VMEM((tokens, columns), BF16),
            pltpu.VMEM((plane, columns), F32),
            pltpu.VMEM((cross - 1, plane, columns), F32),
            pltpu.VMEM((cross - 1, plane, columns), BF16),
            pltpu.VMEM((16, 128) if inside else (tokens, rows_out), BF16),
            pltpu.VMEM((16, 128) if inside else (rows_out, width_out), BF16),
            pltpu.VMEM((outer, block, width_out), F32),
            pltpu.VMEM((inner, outer, block, width_out), BF16),
            pltpu.VMEM((inner - 1, outer, block, width_out), BF16),
            pltpu.VMEM((outer - 1, block, width_out), BF16),
            pltpu.VMEM((outer, inner, block, width_out), BF16),
            pltpu.VMEM((count, tokens, 128), F32),
            pltpu.VMEM((wide, rows_pad, docs_pad), F32),
            pltpu.VMEM((narrow, rows_pad, docs_pad), F32),
            dma((1,)),
            dma((1,)),
            dma((AHEAD,)),
            dma((AHEAD, count,)),
            dma((3,)),
            dma((1,)),
            dma((1,)),
            dma((wide,)),
            dma((parts,)),
            dma((parts,)),
            dma((2,)),
            dma((outer,)),
            dma((outer, chunks,)),
            dma((inner - 1, outer,)),
            dma((inner - 1, outer, chunks,)),
            dma((inner,)),
            dma((inner,)),
            dma((outer,)),
            dma((outer,)),
            dma((outer,)),
            dma((outer,)),
            dma((inner, outer,)),
            dma((inner, outer,)),
            dma((2,)),
            dma((2,)),
            dma((cross,)),
            dma((cross,)),
            dma((cross, cols,)),
            dma((cross, cols,)),
            dma((1,)),
            dma((1,)),
            dma((cols,)),
            dma((cols,)),
            dma((1,)),
            dma((wide,)),
            dma((1,)),
            dma((narrow,)),
        ],
        compiler_params=pltpu.CompilerParams(
            collective_id=0, has_side_effects=True, vmem_limit_bytes=VMEM_LIMIT
        ),
        name="score",
    )(activations, out_grads, basis_in, basis_out, eigenvalues, queries, doc_ids)
    return scores.T


def solution(mesh):
    wide, narrow = mesh.shape["wide"], mesh.shape["narrow"]

    def shards(activations, out_grads, basis_in, basis_out, eigenvalues, queries, doc_ids):
        return score(
            wide, narrow, activations, out_grads, basis_in, basis_out, eigenvalues, queries, doc_ids
        )

    return jax.shard_map(
        shards,
        mesh=mesh,
        in_specs=(
            P("wide", "narrow"),
            P("wide", None),
            P("narrow", "wide"),
            P("wide", "narrow"),
            P("narrow", "wide"),
            P(None, "narrow", "wide"),
            P(),
        ),
        out_specs=P(),
        check_vma=False,
    )
```

```python
import functools

import jax
import jax.numpy as jnp
from jax import lax
from jax.experimental import pallas as pl
from jax.experimental.pallas import tpu as pltpu
from jax.sharding import PartitionSpec as P

DOC_PER = 2
DAMPING = 0.1
F32 = jnp.float32
BF16 = jnp.bfloat16
ANY = pl.BlockSpec(memory_space=pl.ANY)
VMEM_LIMIT = 67_043_328
PIECES = 16
EARLY = 1
BEFORE = 4
AHEAD = 4
DETOUR = 4


def tile_of(size, most):
    return max(t for t in range(128, most + 1, 128) if size % t == 0)


def grid_of(wide):
    outer = max(o for o in (1, 2, 3, 4) if wide % o == 0)
    return outer, wide // outer


def parts_of(rows_out, narrow):
    return max(p for p in range(1, narrow + 1) if narrow % p == 0 and rows_out % (128 * p) == 0)


def fits(depth, columns, tokens, rows_out, width_out):
    return max(tokens, rows_out) <= depth and width_out + rows_out <= columns


def orders(outer):
    order = []
    for z in range(outer):
        inward = 1 if 2 * z < outer - 1 else -1
        order.append(sorted(range(outer), key=lambda p: (abs(p - z), -inward * (p - z))))
    rank = [[order[z].index(p) for p in range(outer)] for z in range(outer)]
    return order, rank


def lookup(table, i, j):
    value = 0
    for a, row in enumerate(table):
        for b, entry in enumerate(row):
            hit = (i == a) if isinstance(j, int) else jnp.logical_and(i == a, j == b)
            if isinstance(j, int) and b != j:
                continue
            value = value + jnp.where(hit, entry, 0)
    return value


def remote(src, dst, send, recv, device):
    return pltpu.make_async_remote_copy(
        src_ref=src,
        dst_ref=dst,
        send_sem=send,
        recv_sem=recv,
        device_id=device,
        device_id_type=pl.DeviceIdType.MESH,
    )


def greet(wide, narrow):
    w, n = lax.axis_index("wide"), lax.axis_index("narrow")
    barrier = pltpu.get_barrier_semaphore()
    for d in range(1, wide):
        pl.semaphore_signal(
            barrier, inc=1, device_id={"wide": lax.rem(w + d, wide)}, device_id_type=pl.DeviceIdType.MESH
        )
    for d in range(1, narrow):
        pl.semaphore_signal(
            barrier, inc=1, device_id={"narrow": lax.rem(n + d, narrow)}, device_id_type=pl.DeviceIdType.MESH
        )

    def met():
        pl.semaphore_wait(barrier, wide + narrow - 2)

    return met


def score_kernel(
    wide, narrow, docs, acts, grads, basis_in, basis_out, eigenvalues, queries, ids, out,
    pre, basis, acts_all, total, acts_done, core_recv, cross_recv, late_recv,
    rows_spare, weights_spare, grads_own, grads_send, first_recv, second_recv, grads_all, lanes, held, across,
    own_sem, out_sem, eig_sem, query_sem, basis_sem, rows_sem, a2a_s, a2a_r, part_s, part_r,
    up_s, fwd_s, z_r, x_s, x_r, y_s, y_r, first_s, first_r, second_s, second_r, gz_s, gz_r, gy_s, gy_r,
    core_s, core_r, cross_s, cross_r, late_s, late_r, done_s, done_r, share_s, share_r, lshare_s, lshare_r,
    send_w, recv_w, send_n, recv_n,
):
    outer, inner = grid_of(wide)
    order, rank = orders(outer)
    cross = narrow // 2
    w, n = lax.axis_index("wide"), lax.axis_index("narrow")
    wo, wi = w // inner, lax.rem(w, inner)
    nx, nc = n // 2, lax.rem(n, 2)
    block, depth_all = acts.shape
    depth, columns = basis.shape[1:]
    chunks = depth_all // depth
    plane = inner * block
    rows_out, width_out = basis_out.shape
    count, width, _ = queries.shape
    slot_plane = [lookup(order, wo, s) for s in range(outer)]

    def side_peer(e):
        return {"wide": wo * inner + lax.rem(wi + e, inner)}

    def line_at(z):
        return {"wide": z * inner + wi}

    def cut(c):
        return pl.ds(pl.multiple_of(c * depth, 128), depth)

    def rows(slot, y):
        return pl.ds(pl.multiple_of(slot * plane + y * block, block), block)

    piece = width // PIECES

    def piece_rows(k, q):
        return pl.ds(pl.multiple_of(q * width + k * piece, 16), piece)

    def eig_rows(k):
        return 1, pl.ds(pl.multiple_of(lax.rem(k, AHEAD) * piece, 16), piece)

    def eig_copy(k):
        slot, at = eig_rows(k)
        return pltpu.make_async_copy(
            eigenvalues.at[pl.ds(pl.multiple_of(k * piece, 16), piece)], basis.at[slot, at], eig_sem.at[lax.rem(k, AHEAD)]
        )

    def query_copy(k, q):
        return pltpu.make_async_copy(
            queries.at[q, pl.ds(pl.multiple_of(k * piece, 16), piece)],
            pre.at[piece_rows(k, q)],
            query_sem.at[lax.rem(k, AHEAD), q],
        )

    def basis_copy(i):
        slot = lax.rem(i, 3)
        return pltpu.make_async_copy(basis_in.at[cut(lax.rem(i, chunks))], basis.at[slot], basis_sem.at[slot])

    if fits(depth, columns, block * wide, rows_out, width_out):
        weights_out = basis.at[2, pl.ds(0, rows_out), pl.ds(0, width_out)]
        rows_held = basis.at[2, pl.ds(0, block * wide), pl.ds(width_out, rows_out)]
    else:
        weights_out, rows_held = weights_spare, rows_spare
    fetch_out = pltpu.make_async_copy(basis_out, weights_out, out_sem.at[0])

    own_acts = pltpu.make_async_copy(acts, acts_all.at[rows(0, wi)], own_sem.at[0])

    parts = parts_of(rows_out, narrow)
    part, base = lax.rem(n, parts), n // parts * parts
    span = rows_out // parts

    def part_cols(to, p):
        return pl.ds(pl.multiple_of(to * rows_out + p * span, 128), span)

    def held_cols(p):
        return pl.ds(pl.multiple_of(p * span, 128), span)

    def held_rows(source):
        o, i = source // inner, lax.rem(source, inner)
        return pl.ds(pl.multiple_of((i * outer + o) * block, block), block)

    own_rows = pltpu.make_async_copy(
        grads.at[:, part_cols(w, part)], rows_held.at[held_rows(w), held_cols(part)], rows_sem.at[0]
    )

    met = greet(wide, narrow)
    own_rows.start()

    def fetch_piece(k):
        eig_copy(k).start()
        for q in range(count):
            query_copy(k, q).start()

    for k in range(AHEAD - 1):
        fetch_piece(k)

    strip = 32

    def precondition(k):
        @pl.when(k + AHEAD - 1 < PIECES)
        def _():
            fetch_piece(k + AHEAD - 1)

        eig_copy(k).wait()
        for q in range(count):
            query_copy(k, q).wait()
        slot, start = 1, lax.rem(k, AHEAD) * piece

        def strip_of(r, carry):
            at = pl.ds(pl.multiple_of(start + r * strip, strip), strip)
            scale = 1.0 / (basis[slot, at].astype(F32) + DAMPING)
            for q in range(count):
                here = pl.ds(pl.multiple_of(q * width + k * piece + r * strip, strip), strip)
                pre[here] = (pre[here].astype(F32) * scale).astype(BF16)
            return carry

        lax.fori_loop(0, piece // strip, strip_of, 0)

    for k in range(EARLY):
        precondition(k)
    met()

    def swap(d):
        to = lax.rem(w + d, wide)
        return remote(
            grads.at[:, part_cols(to, part)], rows_held.at[held_rows(w), held_cols(part)],
            a2a_s.at[0], a2a_r.at[d], {"wide": to},
        )

    def part_copy(j):
        return remote(
            rows_held.at[:, held_cols(part)], rows_held.at[:, held_cols(part)],
            part_s.at[j], part_r.at[j], {"narrow": base + lax.rem(part + j, parts)},
        )

    def own_line(c, up):
        to = wo + 1 if up else wo - 1
        slot = lookup(rank, to, wo)
        return remote(
            acts.at[:, cut(c)], acts_all.at[rows(slot, wi), cut(c)], up_s.at[int(up)], z_r.at[slot, c], line_at(to)
        )

    def line_wait(s, c):
        return remote(
            acts.at[:, cut(c)], acts_all.at[rows(s, wi), cut(c)], fwd_s.at[s], z_r.at[s, c], line_at(wo)
        )

    def onward(s):
        above = slot_plane[s] > wo
        to = jnp.where(above, wo - 1, wo + 1)
        return to, jnp.logical_and(to >= 0, to < outer)

    def forward(s, c):
        to, _ = onward(s)
        slot = lookup(rank, to, slot_plane[s])
        return remote(
            acts_all.at[rows(s, wi), cut(c)], acts_all.at[rows(slot, wi), cut(c)],
            fwd_s.at[s], z_r.at[slot, c], line_at(to),
        )

    def side_copy(e, s, c):
        source = acts.at[:, cut(c)] if s == 0 else acts_all.at[rows(s, wi), cut(c)]
        return remote(source, acts_all.at[rows(s, wi), cut(c)], y_s.at[e - 1, s], y_r.at[e - 1, s, c], side_peer(e))

    bent = DETOUR if inner == 2 else 0
    amid = jnp.logical_and(wo > 0, wo < outer - 1)

    def arrive(s, c):
        line_wait(s, c).wait_recv()
        _, more = onward(s)

        @pl.when(more)
        def _():
            forward(s, c).start()

    other = 1 - wi

    def detour(s, c):
        if s == 0:
            to, source = jnp.where(wo == 0, 1, outer - 2), wo
        else:
            (to, _), source = onward(s), slot_plane[s]
        slot = lookup(rank, to, source)
        return remote(
            acts_all.at[rows(s, other), cut(c)], acts_all.at[rows(slot, other), cut(c)],
            x_s.at[s], x_r.at[slot, c], line_at(to),
        )

    def detour_wait(s, c):
        here = acts_all.at[rows(s, other), cut(c)]
        remote(here, here, x_s.at[s], x_r.at[s, c], line_at(wo)).wait_recv()

    def across_side(s, c):
        for e in range(1, inner):
            side_copy(e, s, c).start()

    for d in range(1, wide):
        swap(d).start()

    def begin(c, carry):
        for e in range(1, inner):
            side_copy(e, 0, c).start()

        @pl.when(wo + 1 < outer)
        def _():
            own_line(c, True).start()

        @pl.when(wo > 0)
        def _():
            own_line(c, False).start()

        return carry

    lax.fori_loop(0, chunks, begin, 0)

    wt = tile_of(width_out, 512)

    def grads_tile(k, carry):
        at = pl.ds(pl.multiple_of(k * wt, 128), wt)
        right = weights_out[:, at]

        def left(i):
            return rows_held[pl.ds(pl.multiple_of(i * outer * block, block), outer * block), :]

        own = jnp.dot(left(wi), right, preferred_element_type=F32)
        grads_own[:, :, at] = own.reshape(outer, block, wt)
        for e in range(1, inner):
            i = lax.rem(wi + e, inner)
            other = jnp.dot(left(i), right, preferred_element_type=F32).astype(BF16)
            grads_send[i, :, :, at] = other.reshape(outer, block, wt)
        return carry

    def first(e):
        return remote(
            grads_send.at[lax.rem(wi + e, inner)], first_recv.at[e - 1], first_s.at[e], first_r.at[e], side_peer(e)
        )

    def second(d):
        to = lax.rem(wo + d, outer)
        return remote(
            grads_send.at[wi, to], second_recv.at[d - 1], second_s.at[d], second_r.at[d], line_at(to)
        )

    def partial_grads():
        fetch_out.wait()
        for j in range(1, parts):
            part_copy(j).wait_recv()
        lax.fori_loop(0, width_out // wt, grads_tile, 0)
        for j in range(1, parts):
            part_copy(j).wait_send()
        basis_copy(2).start()

    for k in range(EARLY, BEFORE):
        precondition(k)
    per_turn = pl.cdiv(PIECES - BEFORE, chunks - 1)

    def turn_one(c, carry):
        for j in range(per_turn):
            k = BEFORE + c * per_turn + j

            @pl.when(k < PIECES)
            def _():
                precondition(k)

            @pl.when(k == PIECES - AHEAD + 1)
            def _():
                basis_copy(0).start()

            @pl.when(k == PIECES - 1)
            def _():
                basis_copy(1).start()

        arrive(1, c)
        across_side(1, c)

        @pl.when(amid)
        def _():
            arrive(2, c)

        @pl.when(c == 0)
        def _():
            fetch_out.start()
            own_acts.start()

        if bent:

            @pl.when(jnp.logical_and(jnp.logical_not(amid), c < bent))
            def _():
                side_copy(1, 0, c).wait_recv()
                detour(0, c).start()

        @pl.when(c == max(chunks - 5, 0))
        def _():
            own_rows.wait()
            for d in range(1, wide):
                swap(d).wait_recv()
            for j in range(1, parts):
                part_copy(j).start()

        @pl.when(c == chunks - 2)
        def _():
            partial_grads()

        return carry

    lax.fori_loop(0, chunks, turn_one, 0)
    for e in range(1, inner):
        first(e).start()

    pair = 2 * plane
    ct = tile_of(columns, 1792)

    def rotate(g, c):
        i = g * chunks + c
        basis_copy(i).wait()
        slot = lax.rem(i, 3)

        def tile(k, carry):
            at = pl.ds(pl.multiple_of(k * ct, 128), ct)
            value = jnp.dot(
                acts_all[g * pair : (g + 1) * pair, cut(c)], basis[slot, :, at], preferred_element_type=F32
            )

            @pl.when(c == 0)
            def _():
                total[:, at] = value

            @pl.when(c > 0)
            def _():
                total[:, at] += value

            return carry

        lax.fori_loop(0, columns // ct, tile, 0)

        @pl.when(i + 3 < 2 * chunks)
        def _():
            basis_copy(i + 3).start()

    def relay_two(c):
        @pl.when(jnp.logical_not(amid))
        def _():
            arrive(2, c)

        straight = jnp.logical_not(jnp.logical_and(amid, c < bent))

        @pl.when(straight)
        def _():
            across_side(2, c)

        @pl.when(amid)
        def _():
            arrive(3, c)

        if bent:

            @pl.when(jnp.logical_not(straight))
            def _():
                detour_wait(2, c)
                detour(2, c).start()

    def turn_two(c, carry):
        for j in range(2):
            ahead = 2 * c + j

            @pl.when(ahead < chunks)
            def _():
                relay_two(ahead)

        @pl.when(jnp.logical_or(amid, c >= bent))
        def _():
            for e in range(1, inner):
                side_copy(e, 0, c).wait_recv()

        if bent:
            late = c - (chunks - bent)

            @pl.when(jnp.logical_and(amid, late >= 0))
            def _():
                detour_wait(3, late)
                detour(3, late).start()

        for e in range(1, inner):
            side_copy(e, 1, c).wait_recv()
        rotate(0, c)
        return carry

    own_acts.wait()
    lax.fori_loop(0, chunks, turn_two, 0)

    partner = {"narrow": nx * 2 + (1 - nc)}
    mine = pl.ds(pl.multiple_of(nc * plane, plane), plane)
    theirs = pl.ds(pl.multiple_of((1 - nc) * plane, plane), plane)
    cols = 7 if columns % 896 == 0 else 1
    cw = columns // cols
    share = plane // cross

    def lane(k):
        return pl.ds(pl.multiple_of(k * cw, 128), cw)

    def cross_peer(d):
        return {"narrow": lax.rem(nx + d, cross) * 2 + nc}

    def core_copy(g):
        return remote(total.at[theirs], core_recv, core_s.at[g], core_r.at[g], partner)

    def cross_copy(d):
        to = lax.rem(nx + d, cross)
        return remote(
            core_recv.at[pl.ds(pl.multiple_of(to * share, share), share)],
            cross_recv.at[d - 1], cross_s.at[d], cross_r.at[d], cross_peer(d),
        )

    def done_rows(g):
        return pl.ds(pl.multiple_of((2 * g + nc) * plane, plane), plane)

    def share_rows(x):
        return pl.ds(pl.multiple_of(nc * plane + x * share, share), share)

    def done_copy(d):
        here = acts_done.at[share_rows(nx)]
        return remote(here, here, done_s.at[d], done_r.at[d], cross_peer(d))

    def last_copy(d):
        here = acts_done.at[share_rows(lax.rem(nx + cross - d, cross))]
        return remote(here, here, share_s.at[d], share_r.at[d], partner)

    def late_copy(d, k):
        return remote(
            acts_done.at[done_rows(1), lane(k)], late_recv.at[d - 1, :, lane(k)], late_s.at[d, k], late_r.at[d, k], cross_peer(d)
        )

    def late_share(k):
        here = acts_done.at[done_rows(1), lane(k)]
        return remote(here, here, lshare_s.at[k], lshare_r.at[k], partner)

    core_copy(0).start()
    core_copy(0).wait_recv()

    def core_sum(k, carry):
        core_recv[:, lane(k)] += total[mine, lane(k)]
        return carry

    lax.fori_loop(0, cols, core_sum, 0)
    for d in range(1, cross):
        cross_copy(d).start()

    def turn_three(c, carry):
        @pl.when(jnp.logical_not(amid))
        def _():
            arrive(3, c)

        @pl.when(c >= bent)
        def _():
            across_side(3, c)

        return carry

    lax.fori_loop(0, chunks, turn_three, 0)

    for e in range(1, inner):
        first(e).wait_recv()
    for o in range(outer):
        value = grads_own[o]
        for e in range(1, inner):
            value = value + first_recv[e - 1, o].astype(F32)
        grads_own[o] = value
        grads_send[wi, o] = value.astype(BF16)
    for d in range(1, outer):
        second(d).start()

    def group_shares():
        for d in range(1, cross):
            cross_copy(d).wait()
        here = pl.ds(pl.multiple_of(nx * share, share), share)

        def cross_sum(k, carry):
            value = core_recv[here, lane(k)]
            for d in range(1, cross):
                value = value + cross_recv[d - 1, :, lane(k)]
            acts_done[share_rows(nx), lane(k)] = value.astype(BF16)
            return carry

        lax.fori_loop(0, cols, cross_sum, 0)
        for d in range(1, cross):
            done_copy(d).start()
        last_copy(0).start()

    def group_done():
        for d in range(1, cross):
            done_copy(d).wait_recv()
            last_copy(d).start()

    def gline(d):
        to = lax.rem(wo + d, outer)
        slot = lookup(rank, to, wo)
        return remote(grads_all.at[0, wi], grads_all.at[slot, wi], gz_s.at[d], gz_r.at[slot], line_at(to))

    def gline_wait(s):
        return remote(grads_all.at[0, wi], grads_all.at[s, wi], gz_s.at[s], gz_r.at[s], line_at(wo))

    def gside(e, s):
        return remote(
            grads_all.at[s, wi], grads_all.at[s, wi], gy_s.at[e, s], gy_r.at[e, s], side_peer(e)
        )

    core_copy(0).wait_send()

    def grads_done():
        for d in range(1, outer):
            second(d).wait_recv()
        value = grads_own[wo]
        for d in range(1, outer):
            value = value + second_recv[d - 1].astype(F32)
        grads_all[0, wi] = value.astype(BF16)

        for d in range(1, outer):
            gline(d).start()
        for e in range(1, inner):
            gside(e, 0).start()

    def turn_four(c, carry):
        @pl.when(jnp.logical_not(jnp.logical_and(amid, c < bent)))
        def _():
            for e in range(1, inner):
                side_copy(e, 2, c).wait_recv()

        @pl.when(c >= bent)
        def _():
            for e in range(1, inner):
                side_copy(e, 3, c).wait_recv()

        if bent:

            @pl.when(jnp.logical_and(jnp.logical_not(amid), c < bent))
            def _():
                detour_wait(3, c)

        rotate(1, c)

        @pl.when(c == jnp.where(amid, chunks // 2 + 1, chunks // 2 - 1))
        def _():
            group_shares()

        @pl.when(c == jnp.where(amid, chunks // 2 + 1, chunks - 2))
        def _():
            grads_done()

        return carry

    lax.fori_loop(0, chunks, turn_four, 0)
    group_done()
    last_copy(0).wait_recv()
    core_copy(1).start()

    def grads_across(s):
        gline_wait(s).wait_recv()
        for e in range(1, inner):
            gside(e, s).start()

    core_copy(1).wait_recv()

    def late_sum(k, carry):
        value = total[mine, lane(k)] + core_recv[:, lane(k)]
        total[mine, lane(k)] = value
        acts_done[done_rows(1), lane(k)] = value.astype(BF16)
        for d in range(1, cross):
            late_copy(d, k).start()
        return carry

    lax.fori_loop(0, cols, late_sum, 0)
    for s in range(1, outer):
        grads_across(s)

    lanes[...] = jnp.zeros_like(lanes)

    def mix(g, k):
        left = grads_all[2 * g : 2 * g + 2].reshape(pair, width)
        here = slice(g * pair, (g + 1) * pair)
        for q in range(count):
            mixed = jnp.dot(left, pre[q * width : (q + 1) * width, lane(k)], preferred_element_type=F32)
            right = acts_done[here, lane(k)].astype(F32)
            value = jnp.zeros((pair, 128), F32)
            for j in range(cw // 128):
                value = value + mixed[:, j * 128 : (j + 1) * 128] * right[:, j * 128 : (j + 1) * 128]
            for h in range(2):
                there = pl.ds(pl.multiple_of(slot_plane[2 * g + h] * plane, plane), plane)
                lanes[q, there] += value[h * plane : (h + 1) * plane]

    for d in range(1, cross):
        last_copy(d).wait_recv()
    for e in range(1, inner):
        for s in (0, 1):
            gside(e, s).wait_recv()

    def mix_early(k, carry):
        mix(0, k)
        return carry

    lax.fori_loop(0, cols, mix_early, 0)

    def late_done(k):
        for d in range(1, cross):
            late_copy(d, k).wait()
        value = total[mine, lane(k)]
        for d in range(1, cross):
            value = value + late_recv[d - 1, :, lane(k)].astype(F32)
        acts_done[done_rows(1), lane(k)] = value.astype(BF16)
        late_share(k).start()

    def late_turn(k, carry):
        late_done(k)
        return carry

    lax.fori_loop(0, cols, late_turn, 0)
    for e in range(1, inner):
        for s in (2, 3):
            gside(e, s).wait_recv()

    def mix_late(k, carry):
        late_share(k).wait_recv()
        mix(1, k)
        return carry

    lax.fori_loop(0, cols, mix_late, 0)

    _, rows_pad, docs_pad = across.shape
    row = lax.broadcasted_iota(jnp.int32, (rows_pad, docs_pad), 0)
    value = jnp.zeros((rows_pad, docs_pad), F32)
    tokens = block * wide
    named = jnp.broadcast_to(ids[...].reshape(1, tokens), (docs_pad, tokens))
    member = (named == lax.broadcasted_iota(jnp.int32, (docs_pad, tokens), 0)).astype(F32)
    for q in range(count):
        doc_lanes = jnp.dot(member, lanes[q], precision=lax.Precision.HIGHEST, preferred_element_type=F32)
        value = jnp.where(row == q, jnp.sum(doc_lanes, axis=1)[None, :], value)
    across[n] = value

    def over_narrow(d):
        return remote(across.at[n], across.at[n], send_n.at[0], recv_n.at[d], {"narrow": lax.rem(n + d, narrow)})

    def over_wide(d):
        return remote(held.at[w], held.at[w], send_w.at[0], recv_w.at[d], {"wide": lax.rem(w + d, wide)})

    for d in range(1, narrow):
        over_narrow(d).start()
    for d in range(1, narrow):
        over_narrow(d).wait_recv()
    value = across[0]
    for d in range(1, narrow):
        value = value + across[d]
    held[w] = value
    for d in range(1, wide):
        over_wide(d).start()
    for d in range(1, wide):
        over_wide(d).wait_recv()
    value = held[0]
    for d in range(1, wide):
        value = value + held[d]
    out[...] = value[: out.shape[0], : out.shape[1]]

    def left(source, sem):
        pltpu.make_async_copy(source, source, sem).wait()

    left(rows_held.at[pl.ds(0, (wide - 1) * block), held_cols(0)], a2a_s.at[0])
    row_block = acts_all.at[rows(0, wi)]

    @pl.when(wo + 1 < outer)
    def _():
        left(row_block, up_s.at[1])

    @pl.when(wo > 0)
    def _():
        left(row_block, up_s.at[0])

    for s in range(1, outer):
        _, more = onward(s)

        @pl.when(more)
        def _():
            left(row_block, fwd_s.at[s])

    for e in range(1, inner):
        for s in (0, 1):
            left(row_block, y_s.at[e - 1, s])
        short = acts_all.at[rows(0, wi), pl.ds(0, (chunks - bent) * depth)]
        left(short, y_s.at[e - 1, 3])

        @pl.when(amid)
        def _():
            left(short, y_s.at[e - 1, 2])

        @pl.when(jnp.logical_not(amid))
        def _():
            left(row_block, y_s.at[e - 1, 2])

    if bent:
        long = acts_all.at[rows(0, wi), pl.ds(0, bent * depth)]

        @pl.when(amid)
        def _():
            left(long, x_s.at[2])
            left(long, x_s.at[3])

        @pl.when(jnp.logical_not(amid))
        def _():
            left(long, x_s.at[0])

    for e in range(1, inner):
        first(e).wait_send()
        for s in range(outer):
            gside(e, s).wait_send()
    for d in range(1, outer):
        second(d).wait_send()
        gline(d).wait_send()
    core_copy(1).wait_send()
    for d in range(cross):
        last_copy(d).wait_send()
    for d in range(1, cross):
        done_copy(d).wait_send()
    for k in range(cols):
        late_share(k).wait_send()
    left(across.at[pl.ds(0, narrow - 1)], send_n.at[0])
    left(held.at[pl.ds(0, wide - 1)], send_w.at[0])


def score(wide, narrow, activations, out_grads, basis_in, basis_out, eigenvalues, queries, doc_ids):
    outer, inner = grid_of(wide)
    cross = narrow // 2
    block, depth_all = activations.shape
    tokens = block * wide
    plane = block * inner
    docs = DOC_PER * wide
    depth = tile_of(depth_all, 1024)
    chunks = depth_all // depth
    columns = basis_in.shape[1]
    rows_out, width_out = basis_out.shape
    count, width, _ = queries.shape
    cols = 7 if columns % 896 == 0 else 1
    parts = parts_of(rows_out, narrow)
    inside = fits(depth, columns, tokens, rows_out, width_out)
    rows_pad, docs_pad = pl.cdiv(count, 8) * 8, pl.cdiv(docs, 128) * 128
    dma = pltpu.SemaphoreType.DMA
    scores = pl.pallas_call(
        functools.partial(score_kernel, wide, narrow, docs),
        out_shape=jax.ShapeDtypeStruct((count, docs), F32),
        in_specs=[ANY] * 6 + [pl.BlockSpec(memory_space=pltpu.VMEM)],
        out_specs=pl.BlockSpec(memory_space=pltpu.VMEM),
        scratch_shapes=[
            pltpu.VMEM((count * width, columns), BF16),
            pltpu.VMEM((3, depth, columns), BF16),
            pltpu.VMEM((tokens, depth_all), BF16),
            pltpu.VMEM((2 * plane, columns), F32),
            pltpu.VMEM((tokens, columns), BF16),
            pltpu.VMEM((plane, columns), F32),
            pltpu.VMEM((cross - 1, plane // cross, columns), F32),
            pltpu.VMEM((cross - 1, plane, columns), BF16),
            pltpu.VMEM((16, 128) if inside else (tokens, rows_out), BF16),
            pltpu.VMEM((16, 128) if inside else (rows_out, width_out), BF16),
            pltpu.VMEM((outer, block, width_out), F32),
            pltpu.VMEM((inner, outer, block, width_out), BF16),
            pltpu.VMEM((inner - 1, outer, block, width_out), BF16),
            pltpu.VMEM((outer - 1, block, width_out), BF16),
            pltpu.VMEM((outer, inner, block, width_out), BF16),
            pltpu.VMEM((count, tokens, 128), F32),
            pltpu.VMEM((wide, rows_pad, docs_pad), F32),
            pltpu.VMEM((narrow, rows_pad, docs_pad), F32),
            dma((1,)),
            dma((1,)),
            dma((AHEAD,)),
            dma((AHEAD, count,)),
            dma((3,)),
            dma((1,)),
            dma((1,)),
            dma((wide,)),
            dma((parts,)),
            dma((parts,)),
            dma((2,)),
            dma((outer,)),
            dma((outer, chunks)),
            dma((outer,)),
            dma((outer, max(DETOUR, 1))),
            dma((inner - 1, outer,)),
            dma((inner - 1, outer, chunks,)),
            dma((inner,)),
            dma((inner,)),
            dma((outer,)),
            dma((outer,)),
            dma((outer,)),
            dma((outer,)),
            dma((inner, outer,)),
            dma((inner, outer,)),
            dma((2,)),
            dma((2,)),
            dma((cross,)),
            dma((cross,)),
            dma((cross, cols,)),
            dma((cross, cols,)),
            dma((cross,)),
            dma((cross,)),
            dma((cross,)),
            dma((cross,)),
            dma((cols,)),
            dma((cols,)),
            dma((1,)),
            dma((wide,)),
            dma((1,)),
            dma((narrow,)),
        ],
        compiler_params=pltpu.CompilerParams(
            collective_id=0, has_side_effects=True, vmem_limit_bytes=VMEM_LIMIT
        ),
        name="score",
    )(activations, out_grads, basis_in, basis_out, eigenvalues, queries, doc_ids)
    return scores.T


def solution(mesh):
    wide, narrow = mesh.shape["wide"], mesh.shape["narrow"]

    def shards(activations, out_grads, basis_in, basis_out, eigenvalues, queries, doc_ids):
        return score(
            wide, narrow, activations, out_grads, basis_in, basis_out, eigenvalues, queries, doc_ids
        )

    return jax.shard_map(
        shards,
        mesh=mesh,
        in_specs=(
            P("wide", "narrow"),
            P("wide", None),
            P("narrow", "wide"),
            P("wide", "narrow"),
            P("narrow", "wide"),
            P(None, "narrow", "wide"),
            P(),
        ),
        out_specs=P(),
        check_vma=False,
    )
```

```python
import functools

import jax
import jax.numpy as jnp
from jax import lax
from jax.experimental import pallas as pl
from jax.experimental.pallas import tpu as pltpu
from jax.sharding import PartitionSpec as P

DOC_PER = 2
DAMPING = 0.1
F32 = jnp.float32
BF16 = jnp.bfloat16
ANY = pl.BlockSpec(memory_space=pl.ANY)
VMEM_LIMIT = 67_043_328
PIECES = 16
EARLY = 1
BEFORE = 4
AHEAD = 4
DETOUR = 3


def tile_of(size, most):
    return max(t for t in range(128, most + 1, 128) if size % t == 0)


def grid_of(wide):
    outer = max(o for o in (1, 2, 3, 4) if wide % o == 0)
    return outer, wide // outer


def parts_of(rows_out, narrow):
    return max(p for p in range(1, narrow + 1) if narrow % p == 0 and rows_out % (128 * p) == 0)


def fits(depth, columns, tokens, rows_out, width_out):
    return max(tokens, rows_out) <= depth and width_out + rows_out <= columns


def orders(outer):
    order = []
    for z in range(outer):
        inward = 1 if 2 * z < outer - 1 else -1
        order.append(sorted(range(outer), key=lambda p: (abs(p - z), -inward * (p - z))))
    rank = [[order[z].index(p) for p in range(outer)] for z in range(outer)]
    return order, rank


def lookup(table, i, j):
    value = 0
    for a, row in enumerate(table):
        for b, entry in enumerate(row):
            hit = (i == a) if isinstance(j, int) else jnp.logical_and(i == a, j == b)
            if isinstance(j, int) and b != j:
                continue
            value = value + jnp.where(hit, entry, 0)
    return value


def remote(src, dst, send, recv, device):
    return pltpu.make_async_remote_copy(
        src_ref=src,
        dst_ref=dst,
        send_sem=send,
        recv_sem=recv,
        device_id=device,
        device_id_type=pl.DeviceIdType.MESH,
    )


def greet(wide, narrow):
    w, n = lax.axis_index("wide"), lax.axis_index("narrow")
    barrier = pltpu.get_barrier_semaphore()
    for d in range(1, wide):
        pl.semaphore_signal(
            barrier, inc=1, device_id={"wide": lax.rem(w + d, wide)}, device_id_type=pl.DeviceIdType.MESH
        )
    for d in range(1, narrow):
        pl.semaphore_signal(
            barrier, inc=1, device_id={"narrow": lax.rem(n + d, narrow)}, device_id_type=pl.DeviceIdType.MESH
        )

    def met():
        pl.semaphore_wait(barrier, wide + narrow - 2)

    return met


def score_kernel(
    wide, narrow, docs, acts, grads, basis_in, basis_out, eigenvalues, queries, ids, out,
    pre, basis, acts_all, total, acts_done, core_recv, cross_recv,
    rows_spare, weights_spare, grads_own, grads_send, first_recv, second_recv, grads_all, lanes, held, across,
    own_sem, out_sem, eig_sem, query_sem, basis_sem, rows_sem, a2a_s, a2a_r, part_s, part_r,
    up_s, fwd_s, z_r, x_s, x_r, y_s, y_r, first_s, first_r, second_s, second_r, gz_s, gz_r, gy_s, gy_r,
    core_s, core_r, cross_s, cross_r, late_s, late_r, spread_s, spread_r, done_s, done_r, share_s, share_r, lshare_s, lshare_r,
    send_w, recv_w, send_n, recv_n,
):
    outer, inner = grid_of(wide)
    order, rank = orders(outer)
    cross = narrow // 2
    w, n = lax.axis_index("wide"), lax.axis_index("narrow")
    wo, wi = w // inner, lax.rem(w, inner)
    nx, nc = n // 2, lax.rem(n, 2)
    block, depth_all = acts.shape
    depth, columns = basis.shape[1:]
    chunks = depth_all // depth
    plane = inner * block
    rows_out, width_out = basis_out.shape
    count, width, _ = queries.shape
    slot_plane = [lookup(order, wo, s) for s in range(outer)]

    def side_peer(e):
        return {"wide": wo * inner + lax.rem(wi + e, inner)}

    def line_at(z):
        return {"wide": z * inner + wi}

    def cut(c):
        return pl.ds(pl.multiple_of(c * depth, 128), depth)

    def rows(slot, y):
        return pl.ds(pl.multiple_of(slot * plane + y * block, block), block)

    piece = width // PIECES

    def piece_rows(k, q):
        return pl.ds(pl.multiple_of(q * width + k * piece, 16), piece)

    def eig_rows(k):
        return 1, pl.ds(pl.multiple_of(lax.rem(k, AHEAD) * piece, 16), piece)

    def eig_copy(k):
        slot, at = eig_rows(k)
        return pltpu.make_async_copy(
            eigenvalues.at[pl.ds(pl.multiple_of(k * piece, 16), piece)], basis.at[slot, at], eig_sem.at[lax.rem(k, AHEAD)]
        )

    def query_copy(k, q):
        return pltpu.make_async_copy(
            queries.at[q, pl.ds(pl.multiple_of(k * piece, 16), piece)],
            pre.at[piece_rows(k, q)],
            query_sem.at[lax.rem(k, AHEAD), q],
        )

    def basis_copy(i):
        slot = lax.rem(i, 3)
        return pltpu.make_async_copy(basis_in.at[cut(lax.rem(i, chunks))], basis.at[slot], basis_sem.at[slot])

    if fits(depth, columns, block * wide, rows_out, width_out):
        weights_out = basis.at[2, pl.ds(0, rows_out), pl.ds(0, width_out)]
        rows_held = basis.at[2, pl.ds(0, block * wide), pl.ds(width_out, rows_out)]
    else:
        weights_out, rows_held = weights_spare, rows_spare
    fetch_out = pltpu.make_async_copy(basis_out, weights_out, out_sem.at[0])

    own_acts = pltpu.make_async_copy(acts, acts_all.at[rows(0, wi)], own_sem.at[0])

    parts = parts_of(rows_out, narrow)
    part, base = lax.rem(n, parts), n // parts * parts
    span = rows_out // parts

    def part_cols(to, p):
        return pl.ds(pl.multiple_of(to * rows_out + p * span, 128), span)

    def held_cols(p):
        return pl.ds(pl.multiple_of(p * span, 128), span)

    def held_rows(source):
        o, i = source // inner, lax.rem(source, inner)
        return pl.ds(pl.multiple_of((i * outer + o) * block, block), block)

    own_rows = pltpu.make_async_copy(
        grads.at[:, part_cols(w, part)], rows_held.at[held_rows(w), held_cols(part)], rows_sem.at[0]
    )

    def left(source, sem):
        pltpu.make_async_copy(source, source, sem).wait()

    met = greet(wide, narrow)
    own_rows.start()

    def fetch_piece(k):
        eig_copy(k).start()
        for q in range(count):
            query_copy(k, q).start()

    for k in range(AHEAD - 1):
        fetch_piece(k)

    strip = 32

    def precondition(k):
        @pl.when(k + AHEAD - 1 < PIECES)
        def _():
            fetch_piece(k + AHEAD - 1)

        eig_copy(k).wait()
        for q in range(count):
            query_copy(k, q).wait()
        slot, start = 1, lax.rem(k, AHEAD) * piece

        def strip_of(r, carry):
            at = pl.ds(pl.multiple_of(start + r * strip, strip), strip)
            scale = 1.0 / (basis[slot, at].astype(F32) + DAMPING)
            for q in range(count):
                here = pl.ds(pl.multiple_of(q * width + k * piece + r * strip, strip), strip)
                pre[here] = (pre[here].astype(F32) * scale).astype(BF16)
            return carry

        lax.fori_loop(0, piece // strip, strip_of, 0)

    for k in range(EARLY):
        precondition(k)
    met()

    def swap(d):
        to = lax.rem(w + d, wide)
        return remote(
            grads.at[:, part_cols(to, part)], rows_held.at[held_rows(w), held_cols(part)],
            a2a_s.at[0], a2a_r.at[d], {"wide": to},
        )

    def part_copy(j):
        return remote(
            rows_held.at[:, held_cols(part)], rows_held.at[:, held_cols(part)],
            part_s.at[0], part_r.at[j - 1], {"narrow": base + lax.rem(part + j, parts)},
        )

    def own_line(c, up):
        to = wo + 1 if up else wo - 1
        slot = lookup(rank, to, wo)
        return remote(
            acts.at[:, cut(c)], acts_all.at[rows(slot, wi), cut(c)], up_s.at[int(up)], z_r.at[slot, c], line_at(to)
        )

    def line_wait(s, c):
        return remote(
            acts.at[:, cut(c)], acts_all.at[rows(s, wi), cut(c)], fwd_s.at[s], z_r.at[s, c], line_at(wo)
        )

    def onward(s):
        above = slot_plane[s] > wo
        to = jnp.where(above, wo - 1, wo + 1)
        return to, jnp.logical_and(to >= 0, to < outer)

    def forward(s, c):
        to, _ = onward(s)
        slot = lookup(rank, to, slot_plane[s])
        return remote(
            acts_all.at[rows(s, wi), cut(c)], acts_all.at[rows(slot, wi), cut(c)],
            fwd_s.at[s], z_r.at[slot, c], line_at(to),
        )

    def side_copy(e, s, c):
        source = acts.at[:, cut(c)] if s == 0 else acts_all.at[rows(s, wi), cut(c)]
        return remote(source, acts_all.at[rows(s, wi), cut(c)], y_s.at[e - 1, s], y_r.at[e - 1, s, c], side_peer(e))

    bent = DETOUR if inner == 2 else 0
    amid = jnp.logical_and(wo > 0, wo < outer - 1)

    def arrive(s, c):
        line_wait(s, c).wait_recv()
        _, more = onward(s)

        @pl.when(more)
        def _():
            forward(s, c).start()

    other = 1 - wi

    def detour(s, c):
        if s == 0:
            to, source = jnp.where(wo == 0, 1, outer - 2), wo
        else:
            (to, _), source = onward(s), slot_plane[s]
        slot = lookup(rank, to, source)
        return remote(
            acts_all.at[rows(s, other), cut(c)], acts_all.at[rows(slot, other), cut(c)],
            x_s.at[s], x_r.at[slot - 2, c], line_at(to),
        )

    def detour_wait(s, c):
        here = acts_all.at[rows(s, other), cut(c)]
        remote(here, here, x_s.at[s], x_r.at[s - 2, c], line_at(wo)).wait_recv()

    def across_side(s, c):
        for e in range(1, inner):
            side_copy(e, s, c).start()

    for d in range(1, wide):
        swap(d).start()

    def begin(c, carry):
        for e in range(1, inner):
            side_copy(e, 0, c).start()

        @pl.when(wo + 1 < outer)
        def _():
            own_line(c, True).start()

        @pl.when(wo > 0)
        def _():
            own_line(c, False).start()

        return carry

    lax.fori_loop(0, chunks, begin, 0)

    wt = tile_of(width_out, 512)

    def grads_tile(k, carry):
        at = pl.ds(pl.multiple_of(k * wt, 128), wt)
        right = weights_out[:, at]

        def left(i):
            return rows_held[pl.ds(pl.multiple_of(i * outer * block, block), outer * block), :]

        own = jnp.dot(left(wi), right, preferred_element_type=F32)
        grads_own[:, :, at] = own.reshape(outer, block, wt)
        for e in range(1, inner):
            i = lax.rem(wi + e, inner)
            other = jnp.dot(left(i), right, preferred_element_type=F32).astype(BF16)
            grads_send[i, :, :, at] = other.reshape(outer, block, wt)
        return carry

    def first(e):
        return remote(
            grads_send.at[lax.rem(wi + e, inner)], first_recv.at[e - 1], first_s.at[e], first_r.at[e], side_peer(e)
        )

    def second(d):
        to = lax.rem(wo + d, outer)
        return remote(
            grads_send.at[wi, to], second_recv.at[d - 1], second_s.at[0], second_r.at[d - 1], line_at(to)
        )

    def partial_grads():
        fetch_out.wait()
        for j in range(1, parts):
            part_copy(j).wait_recv()
        lax.fori_loop(0, width_out // wt, grads_tile, 0)
        left(rows_held.at[:, pl.ds(0, (parts - 1) * span)], part_s.at[0])
        basis_copy(2).start()

    for k in range(EARLY, BEFORE):
        precondition(k)
    per_turn = pl.cdiv(PIECES - BEFORE, chunks - 1)

    def turn_one(c, carry):
        for j in range(per_turn):
            k = BEFORE + c * per_turn + j

            @pl.when(k < PIECES)
            def _():
                precondition(k)

            @pl.when(k == PIECES - AHEAD + 1)
            def _():
                basis_copy(0).start()

            @pl.when(k == PIECES - 1)
            def _():
                basis_copy(1).start()

        arrive(1, c)
        across_side(1, c)

        @pl.when(amid)
        def _():
            arrive(2, c)

        @pl.when(c == 0)
        def _():
            fetch_out.start()
            own_acts.start()

        if bent:

            @pl.when(jnp.logical_and(jnp.logical_not(amid), c < bent))
            def _():
                side_copy(1, 0, c).wait_recv()
                detour(0, c).start()

        @pl.when(c == max(chunks - 5, 0))
        def _():
            own_rows.wait()
            for d in range(1, wide):
                swap(d).wait_recv()
            for j in range(1, parts):
                part_copy(j).start()

        @pl.when(c == chunks - 2)
        def _():
            partial_grads()

        return carry

    lax.fori_loop(0, chunks, turn_one, 0)
    for e in range(1, inner):
        first(e).start()

    pair = 2 * plane
    ct = tile_of(columns, 1792)

    def rotate(g, c):
        i = g * chunks + c
        basis_copy(i).wait()
        slot = lax.rem(i, 3)

        def tile(k, carry):
            at = pl.ds(pl.multiple_of(k * ct, 128), ct)
            value = jnp.dot(
                acts_all[g * pair : (g + 1) * pair, cut(c)], basis[slot, :, at], preferred_element_type=F32
            )

            @pl.when(c == 0)
            def _():
                total[:, at] = value

            @pl.when(c > 0)
            def _():
                total[:, at] += value

            return carry

        lax.fori_loop(0, columns // ct, tile, 0)

        @pl.when(i + 3 < 2 * chunks)
        def _():
            basis_copy(i + 3).start()

    def relay_two(c):
        @pl.when(jnp.logical_not(amid))
        def _():
            arrive(2, c)

        straight = jnp.logical_not(jnp.logical_and(amid, c < bent))

        @pl.when(straight)
        def _():
            across_side(2, c)

        @pl.when(amid)
        def _():
            arrive(3, c)

        if bent:

            @pl.when(jnp.logical_not(straight))
            def _():
                detour_wait(2, c)
                detour(2, c).start()

    def turn_two(c, carry):
        for j in range(2):
            ahead = 2 * c + j

            @pl.when(ahead < chunks)
            def _():
                relay_two(ahead)

        @pl.when(jnp.logical_or(amid, c >= bent))
        def _():
            for e in range(1, inner):
                side_copy(e, 0, c).wait_recv()

        if bent:
            late = c - (chunks - bent)

            @pl.when(jnp.logical_and(amid, late >= 0))
            def _():
                detour_wait(3, late)
                detour(3, late).start()

        for e in range(1, inner):
            side_copy(e, 1, c).wait_recv()
        rotate(0, c)
        return carry

    own_acts.wait()
    lax.fori_loop(0, chunks, turn_two, 0)

    partner = {"narrow": nx * 2 + (1 - nc)}
    mine = pl.ds(pl.multiple_of(nc * plane, plane), plane)
    theirs = pl.ds(pl.multiple_of((1 - nc) * plane, plane), plane)
    cols = 7 if columns % 896 == 0 else 1
    cw = columns // cols
    share = plane // cross

    def lane(k):
        return pl.ds(pl.multiple_of(k * cw, 128), cw)

    def cross_peer(d):
        return {"narrow": lax.rem(nx + d, cross) * 2 + nc}

    def core_copy(g):
        return remote(total.at[theirs], core_recv, core_s.at[g], core_r.at[g], partner)

    def cross_copy(d):
        to = lax.rem(nx + d, cross)
        return remote(
            core_recv.at[pl.ds(pl.multiple_of(to * share, share), share)],
            cross_recv.at[d - 1], cross_s.at[d], cross_r.at[d], cross_peer(d),
        )

    def share_rows(x):
        return pl.ds(pl.multiple_of(nc * plane + x * share, share), share)

    def done_copy(d):
        here = acts_done.at[share_rows(nx)]
        return remote(here, here, done_s.at[d], done_r.at[d], cross_peer(d))

    def last_copy(d):
        here = acts_done.at[share_rows(lax.rem(nx + cross - d, cross))]
        return remote(here, here, share_s.at[d], share_r.at[d], partner)

    def part_of(x):
        return pl.ds(pl.multiple_of(nc * plane + x * share, share), share)

    def late_rows(x):
        return pl.ds(pl.multiple_of((2 + nc) * plane + x * share, share), share)

    def late_copy(d, k):
        return remote(
            total.at[part_of(lax.rem(nx + d, cross)), lane(k)], cross_recv.at[d - 1, :, lane(k)],
            late_s.at[d - 1], late_r.at[d - 1, k], cross_peer(d),
        )

    def late_spread(d, k):
        here = acts_done.at[late_rows(nx), lane(k)]
        return remote(here, here, spread_s.at[d - 1], spread_r.at[d - 1, k], cross_peer(d))

    def late_share(d, k):
        here = acts_done.at[late_rows(lax.rem(nx + cross - d, cross)), lane(k)]
        return remote(here, here, lshare_s.at[d], lshare_r.at[d, k], partner)

    core_copy(0).start()
    core_copy(0).wait_recv()

    def core_sum(k, carry):
        core_recv[:, lane(k)] += total[mine, lane(k)]
        return carry

    lax.fori_loop(0, cols, core_sum, 0)
    for d in range(1, cross):
        cross_copy(d).start()

    def turn_three(c, carry):
        @pl.when(jnp.logical_not(amid))
        def _():
            arrive(3, c)

        @pl.when(c >= bent)
        def _():
            across_side(3, c)

        return carry

    lax.fori_loop(0, chunks, turn_three, 0)

    for e in range(1, inner):
        first(e).wait_recv()
    for o in range(outer):
        value = grads_own[o]
        for e in range(1, inner):
            value = value + first_recv[e - 1, o].astype(F32)
        grads_own[o] = value
        grads_send[wi, o] = value.astype(BF16)
    for d in range(1, outer):
        second(d).start()

    def group_shares():
        for d in range(1, cross):
            cross_copy(d).wait()
        here = pl.ds(pl.multiple_of(nx * share, share), share)

        def cross_sum(k, carry):
            value = core_recv[here, lane(k)]
            for d in range(1, cross):
                value = value + cross_recv[d - 1, :, lane(k)]
            acts_done[share_rows(nx), lane(k)] = value.astype(BF16)
            return carry

        lax.fori_loop(0, cols, cross_sum, 0)
        for d in range(1, cross):
            done_copy(d).start()
        last_copy(0).start()

    def group_done():
        for d in range(1, cross):
            done_copy(d).wait_recv()
            last_copy(d).start()

    def gline(d):
        to = lax.rem(wo + d, outer)
        slot = lookup(rank, to, wo)
        return remote(grads_all.at[0, wi], grads_all.at[slot, wi], gz_s.at[0], gz_r.at[slot], line_at(to))

    def gline_wait(s):
        return remote(grads_all.at[0, wi], grads_all.at[s, wi], gz_s.at[0], gz_r.at[s], line_at(wo))

    def gside(e, s):
        return remote(
            grads_all.at[s, wi], grads_all.at[s, wi], gy_s.at[e - 1], gy_r.at[e - 1, s], side_peer(e)
        )

    core_copy(0).wait_send()

    def grads_done():
        for d in range(1, outer):
            second(d).wait_recv()
        value = grads_own[wo]
        for d in range(1, outer):
            value = value + second_recv[d - 1].astype(F32)
        grads_all[0, wi] = value.astype(BF16)

        for d in range(1, outer):
            gline(d).start()
        for e in range(1, inner):
            gside(e, 0).start()

    def turn_four(c, carry):
        @pl.when(jnp.logical_not(jnp.logical_and(amid, c < bent)))
        def _():
            for e in range(1, inner):
                side_copy(e, 2, c).wait_recv()

        @pl.when(c >= bent)
        def _():
            for e in range(1, inner):
                side_copy(e, 3, c).wait_recv()

        if bent:

            @pl.when(jnp.logical_and(jnp.logical_not(amid), c < bent))
            def _():
                detour_wait(3, c)

        rotate(1, c)

        @pl.when(c == jnp.where(amid, chunks // 2 + 1, chunks // 2 - 1))
        def _():
            group_shares()

        @pl.when(c == jnp.where(amid, chunks // 2 + 1, chunks - 2))
        def _():
            grads_done()

        return carry

    lax.fori_loop(0, chunks, turn_four, 0)
    group_done()
    last_copy(0).wait_recv()
    core_copy(1).start()

    def grads_across(s):
        gline_wait(s).wait_recv()
        for e in range(1, inner):
            gside(e, s).start()

    core_copy(1).wait_recv()

    def late_sum(k, carry):
        value = total[mine, lane(k)] + core_recv[:, lane(k)]
        total[mine, lane(k)] = value
        for d in range(1, cross):
            late_copy(d, k).start()
        return carry

    lax.fori_loop(0, cols, late_sum, 0)
    for s in range(1, outer):
        grads_across(s)

    lanes[...] = jnp.zeros_like(lanes)

    def mix(g, k):
        left = grads_all[2 * g : 2 * g + 2].reshape(pair, width)
        here = slice(g * pair, (g + 1) * pair)
        for q in range(count):
            mixed = jnp.dot(left, pre[q * width : (q + 1) * width, lane(k)], preferred_element_type=F32)
            right = acts_done[here, lane(k)].astype(F32)
            value = jnp.zeros((pair, 128), F32)
            for j in range(cw // 128):
                value = value + mixed[:, j * 128 : (j + 1) * 128] * right[:, j * 128 : (j + 1) * 128]
            for h in range(2):
                there = pl.ds(pl.multiple_of(slot_plane[2 * g + h] * plane, plane), plane)
                lanes[q, there] += value[h * plane : (h + 1) * plane]

    def late_add(k):
        for d in range(1, cross):
            late_copy(d, k).wait_recv()
        value = total[part_of(nx), lane(k)]
        for d in range(1, cross):
            value = value + cross_recv[d - 1, :, lane(k)]
        acts_done[late_rows(nx), lane(k)] = value.astype(BF16)
        for d in range(1, cross):
            late_spread(d, k).start()
        late_share(0, k).start()

    def late_pass(k):
        for d in range(1, cross):
            late_spread(d, k).wait_recv()
            late_share(d, k).start()

    def late_lead(k, carry):
        late_add(k)
        return carry

    lead = cols // 2
    lax.fori_loop(0, lead, late_lead, 0)
    for d in range(1, cross):
        last_copy(d).wait_recv()
    for e in range(1, inner):
        for s in (0, 1):
            gside(e, s).wait_recv()

    def mix_early(k, carry):
        mix(0, k)

        @pl.when(k >= lead)
        def _():
            late_add(k)

        return carry

    lax.fori_loop(0, cols, mix_early, 0)

    for k in range(min(2, cols)):
        late_pass(k)
    for e in range(1, inner):
        for s in (2, 3):
            gside(e, s).wait_recv()

    def mix_late(k, carry):
        @pl.when(k + 2 < cols)
        def _():
            late_pass(k + 2)

        for d in range(cross):
            late_share(d, k).wait_recv()
        mix(1, k)
        return carry

    lax.fori_loop(0, cols, mix_late, 0)

    _, rows_pad, docs_pad = across.shape
    row = lax.broadcasted_iota(jnp.int32, (rows_pad, docs_pad), 0)
    value = jnp.zeros((rows_pad, docs_pad), F32)
    tokens = block * wide
    named = jnp.broadcast_to(ids[...].reshape(1, tokens), (docs_pad, tokens))
    member = (named == lax.broadcasted_iota(jnp.int32, (docs_pad, tokens), 0)).astype(F32)
    for q in range(count):
        doc_lanes = jnp.dot(member, lanes[q], precision=lax.Precision.HIGHEST, preferred_element_type=F32)
        value = jnp.where(row == q, jnp.sum(doc_lanes, axis=1)[None, :], value)
    across[n] = value

    def over_narrow(d):
        return remote(across.at[n], across.at[n], send_n.at[0], recv_n.at[d], {"narrow": lax.rem(n + d, narrow)})

    def over_wide(d):
        return remote(held.at[w], held.at[w], send_w.at[0], recv_w.at[d], {"wide": lax.rem(w + d, wide)})

    for d in range(1, narrow):
        over_narrow(d).start()
    for d in range(1, narrow):
        over_narrow(d).wait_recv()
    value = across[0]
    for d in range(1, narrow):
        value = value + across[d]
    held[w] = value
    for d in range(1, wide):
        over_wide(d).start()
    for d in range(1, wide):
        over_wide(d).wait_recv()
    value = held[0]
    for d in range(1, wide):
        value = value + held[d]
    out[...] = value[: out.shape[0], : out.shape[1]]

    left(rows_held.at[pl.ds(0, (wide - 1) * block), held_cols(0)], a2a_s.at[0])
    row_block = acts_all.at[rows(0, wi)]

    @pl.when(wo + 1 < outer)
    def _():
        left(row_block, up_s.at[1])

    @pl.when(wo > 0)
    def _():
        left(row_block, up_s.at[0])

    for s in range(1, outer):
        _, more = onward(s)

        @pl.when(more)
        def _():
            left(row_block, fwd_s.at[s])

    for e in range(1, inner):
        for s in (0, 1):
            left(row_block, y_s.at[e - 1, s])
        short = acts_all.at[rows(0, wi), pl.ds(0, (chunks - bent) * depth)]
        left(short, y_s.at[e - 1, 3])

        @pl.when(amid)
        def _():
            left(short, y_s.at[e - 1, 2])

        @pl.when(jnp.logical_not(amid))
        def _():
            left(row_block, y_s.at[e - 1, 2])

    if bent:
        long = acts_all.at[rows(0, wi), pl.ds(0, bent * depth)]

        @pl.when(amid)
        def _():
            left(long, x_s.at[2])
            left(long, x_s.at[3])

        @pl.when(jnp.logical_not(amid))
        def _():
            left(long, x_s.at[0])

    for e in range(1, inner):
        first(e).wait_send()
        left(grads_all.at[:, 0], gy_s.at[e - 1])
    left(second_recv, second_s.at[0])
    left(second_recv, gz_s.at[0])
    core_copy(1).wait_send()
    for d in range(cross):
        last_copy(d).wait_send()
    for d in range(1, cross):
        done_copy(d).wait_send()
    f32_part, bf16_part = total.at[pl.ds(0, share)], acts_done.at[pl.ds(0, share)]
    left(bf16_part, lshare_s.at[0])
    for d in range(1, cross):
        left(f32_part, late_s.at[d - 1])
        left(bf16_part, spread_s.at[d - 1])
        left(bf16_part, lshare_s.at[d])
    left(across.at[pl.ds(0, narrow - 1)], send_n.at[0])
    left(held.at[pl.ds(0, wide - 1)], send_w.at[0])


def score(wide, narrow, activations, out_grads, basis_in, basis_out, eigenvalues, queries, doc_ids):
    outer, inner = grid_of(wide)
    cross = narrow // 2
    block, depth_all = activations.shape
    tokens = block * wide
    plane = block * inner
    docs = DOC_PER * wide
    depth = tile_of(depth_all, 1024)
    chunks = depth_all // depth
    columns = basis_in.shape[1]
    rows_out, width_out = basis_out.shape
    count, width, _ = queries.shape
    cols = 7 if columns % 896 == 0 else 1
    parts = parts_of(rows_out, narrow)
    inside = fits(depth, columns, tokens, rows_out, width_out)
    rows_pad, docs_pad = pl.cdiv(count, 8) * 8, pl.cdiv(docs, 128) * 128
    dma = pltpu.SemaphoreType.DMA
    scores = pl.pallas_call(
        functools.partial(score_kernel, wide, narrow, docs),
        out_shape=jax.ShapeDtypeStruct((count, docs), F32),
        in_specs=[ANY] * 6 + [pl.BlockSpec(memory_space=pltpu.VMEM)],
        out_specs=pl.BlockSpec(memory_space=pltpu.VMEM),
        scratch_shapes=[
            pltpu.VMEM((count * width, columns), BF16),
            pltpu.VMEM((3, depth, columns), BF16),
            pltpu.VMEM((tokens, depth_all), BF16),
            pltpu.VMEM((2 * plane, columns), F32),
            pltpu.VMEM((tokens, columns), BF16),
            pltpu.VMEM((plane, columns), F32),
            pltpu.VMEM((cross - 1, plane // cross, columns), F32),
            pltpu.VMEM((16, 128) if inside else (tokens, rows_out), BF16),
            pltpu.VMEM((16, 128) if inside else (rows_out, width_out), BF16),
            pltpu.VMEM((outer, block, width_out), F32),
            pltpu.VMEM((inner, outer, block, width_out), BF16),
            pltpu.VMEM((inner - 1, outer, block, width_out), BF16),
            pltpu.VMEM((outer - 1, block, width_out), BF16),
            pltpu.VMEM((outer, inner, block, width_out), BF16),
            pltpu.VMEM((count, tokens, 128), F32),
            pltpu.VMEM((wide, rows_pad, docs_pad), F32),
            pltpu.VMEM((narrow, rows_pad, docs_pad), F32),
            dma((1,)),
            dma((1,)),
            dma((AHEAD,)),
            dma((AHEAD, count,)),
            dma((3,)),
            dma((1,)),
            dma((1,)),
            dma((wide,)),
            dma((1,)),
            dma((parts,)),
            dma((2,)),
            dma((outer,)),
            dma((outer, chunks)),
            dma((outer,)),
            dma((2, max(DETOUR, 1))),
            dma((inner - 1, outer,)),
            dma((inner - 1, outer, chunks,)),
            dma((inner,)),
            dma((inner,)),
            dma((1,)),
            dma((outer,)),
            dma((1,)),
            dma((outer,)),
            dma((inner,)),
            dma((inner - 1, outer)),
            dma((2,)),
            dma((2,)),
            dma((cross,)),
            dma((cross,)),
            dma((cross - 1,)),
            dma((cross - 1, cols)),
            dma((cross - 1,)),
            dma((cross - 1, cols)),
            dma((cross,)),
            dma((cross,)),
            dma((cross,)),
            dma((cross,)),
            dma((cross,)),
            dma((cross, cols)),
            dma((1,)),
            dma((wide,)),
            dma((1,)),
            dma((narrow,)),
        ],
        compiler_params=pltpu.CompilerParams(
            collective_id=0, has_side_effects=True, vmem_limit_bytes=VMEM_LIMIT
        ),
        name="score",
    )(activations, out_grads, basis_in, basis_out, eigenvalues, queries, doc_ids)
    return scores.T


def solution(mesh):
    wide, narrow = mesh.shape["wide"], mesh.shape["narrow"]

    def shards(activations, out_grads, basis_in, basis_out, eigenvalues, queries, doc_ids):
        return score(
            wide, narrow, activations, out_grads, basis_in, basis_out, eigenvalues, queries, doc_ids
        )

    return jax.shard_map(
        shards,
        mesh=mesh,
        in_specs=(
            P("wide", "narrow"),
            P("wide", None),
            P("narrow", "wide"),
            P("wide", "narrow"),
            P("narrow", "wide"),
            P(None, "narrow", "wide"),
            P(),
        ),
        out_specs=P(),
        check_vma=False,
    )
```

```python
import functools

import jax
import jax.numpy as jnp
from jax import lax
from jax.experimental import pallas as pl
from jax.experimental.pallas import tpu as pltpu
from jax.sharding import PartitionSpec as P

DOC_PER = 2
DAMPING = 0.1
F32 = jnp.float32
BF16 = jnp.bfloat16
ANY = pl.BlockSpec(memory_space=pl.ANY)
VMEM_LIMIT = 67_043_328
PIECES = 16
EARLY = 1
BEFORE = 4
AHEAD = 5
DETOUR = 3


def tile_of(size, most):
    return max(t for t in range(128, most + 1, 128) if size % t == 0)


def grid_of(wide):
    outer = max(o for o in (1, 2, 3, 4) if wide % o == 0)
    return outer, wide // outer


def parts_of(rows_out, narrow):
    return max(p for p in range(1, narrow + 1) if narrow % p == 0 and rows_out % (128 * p) == 0)


def fits(depth, columns, tokens, rows_out, width_out):
    return max(tokens, rows_out) <= depth and width_out + rows_out <= columns


def orders(outer):
    order = []
    for z in range(outer):
        inward = 1 if 2 * z < outer - 1 else -1
        order.append(sorted(range(outer), key=lambda p: (abs(p - z), -inward * (p - z))))
    rank = [[order[z].index(p) for p in range(outer)] for z in range(outer)]
    return order, rank


def lookup(table, i, j):
    value = 0
    for a, row in enumerate(table):
        for b, entry in enumerate(row):
            hit = (i == a) if isinstance(j, int) else jnp.logical_and(i == a, j == b)
            if isinstance(j, int) and b != j:
                continue
            value = value + jnp.where(hit, entry, 0)
    return value


def remote(src, dst, send, recv, device):
    return pltpu.make_async_remote_copy(
        src_ref=src,
        dst_ref=dst,
        send_sem=send,
        recv_sem=recv,
        device_id=device,
        device_id_type=pl.DeviceIdType.MESH,
    )


def greet(wide, narrow):
    w, n = lax.axis_index("wide"), lax.axis_index("narrow")
    barrier = pltpu.get_barrier_semaphore()
    for d in range(1, wide):
        pl.semaphore_signal(
            barrier, inc=1, device_id={"wide": lax.rem(w + d, wide)}, device_id_type=pl.DeviceIdType.MESH
        )
    for d in range(1, narrow):
        pl.semaphore_signal(
            barrier, inc=1, device_id={"narrow": lax.rem(n + d, narrow)}, device_id_type=pl.DeviceIdType.MESH
        )

    def met():
        pl.semaphore_wait(barrier, wide + narrow - 2)

    return met


def score_kernel(
    wide, narrow, docs, acts, grads, basis_in, basis_out, eigenvalues, queries, ids, out,
    pre, basis, acts_all, total, acts_done, core_recv, cross_recv,
    rows_spare, weights_spare, grads_own, grads_send, first_recv, second_recv, grads_all, lanes, held, across,
    own_sem, out_sem, eig_sem, query_sem, basis_sem, rows_sem, a2a_s, a2a_r, part_s, part_r,
    up_s, fwd_s, z_r, x_s, x_r, y_s, y_r, first_s, first_r, second_s, second_r, gz_s, gz_r, gy_s, gy_r,
    core_s, core_r, cross_s, cross_r, late_s, late_r, spread_s, spread_r, done_s, done_r, share_s, share_r, lshare_s, lshare_r,
    send_w, recv_w, send_n, recv_n,
):
    outer, inner = grid_of(wide)
    order, rank = orders(outer)
    cross = narrow // 2
    w, n = lax.axis_index("wide"), lax.axis_index("narrow")
    wo, wi = w // inner, lax.rem(w, inner)
    nx, nc = n // 2, lax.rem(n, 2)
    block, depth_all = acts.shape
    depth, columns = basis.shape[1:]
    chunks = depth_all // depth
    plane = inner * block
    rows_out, width_out = basis_out.shape
    count, width, _ = queries.shape
    slot_plane = [lookup(order, wo, s) for s in range(outer)]

    def side_peer(e):
        return {"wide": wo * inner + lax.rem(wi + e, inner)}

    def line_at(z):
        return {"wide": z * inner + wi}

    def cut(c):
        return pl.ds(pl.multiple_of(c * depth, 128), depth)

    def rows(slot, y):
        return pl.ds(pl.multiple_of(slot * plane + y * block, block), block)

    piece = width // PIECES

    def piece_rows(k, q):
        return pl.ds(pl.multiple_of(q * width + k * piece, 16), piece)

    def eig_rows(k):
        return 1, pl.ds(pl.multiple_of(lax.rem(k, AHEAD) * piece, 16), piece)

    def eig_copy(k):
        slot, at = eig_rows(k)
        return pltpu.make_async_copy(
            eigenvalues.at[pl.ds(pl.multiple_of(k * piece, 16), piece)], basis.at[slot, at], eig_sem.at[lax.rem(k, AHEAD)]
        )

    def query_copy(k, q):
        return pltpu.make_async_copy(
            queries.at[q, pl.ds(pl.multiple_of(k * piece, 16), piece)],
            pre.at[piece_rows(k, q)],
            query_sem.at[lax.rem(k, AHEAD), q],
        )

    def basis_copy(i):
        slot = lax.rem(i, 3)
        return pltpu.make_async_copy(basis_in.at[cut(lax.rem(i, chunks))], basis.at[slot], basis_sem.at[slot])

    if fits(depth, columns, block * wide, rows_out, width_out):
        weights_out = basis.at[2, pl.ds(0, rows_out), pl.ds(0, width_out)]
        rows_held = basis.at[2, pl.ds(0, block * wide), pl.ds(width_out, rows_out)]
    else:
        weights_out, rows_held = weights_spare, rows_spare
    fetch_out = pltpu.make_async_copy(basis_out, weights_out, out_sem.at[0])

    own_acts = pltpu.make_async_copy(acts, acts_all.at[rows(0, wi)], own_sem.at[0])

    parts = parts_of(rows_out, narrow)
    part, base = lax.rem(n, parts), n // parts * parts
    span = rows_out // parts

    def part_cols(to, p):
        return pl.ds(pl.multiple_of(to * rows_out + p * span, 128), span)

    def held_cols(p):
        return pl.ds(pl.multiple_of(p * span, 128), span)

    def held_rows(source):
        o, i = source // inner, lax.rem(source, inner)
        return pl.ds(pl.multiple_of((i * outer + o) * block, block), block)

    own_rows = pltpu.make_async_copy(
        grads.at[:, part_cols(w, part)], rows_held.at[held_rows(w), held_cols(part)], rows_sem.at[0]
    )

    def left(source, sem):
        pltpu.make_async_copy(source, source, sem).wait()

    met = greet(wide, narrow)
    own_rows.start()

    def fetch_piece(k):
        eig_copy(k).start()
        for q in range(count):
            query_copy(k, q).start()

    for k in range(AHEAD - 1):
        fetch_piece(k)

    strip = 32

    def precondition(k):
        @pl.when(k + AHEAD - 1 < PIECES)
        def _():
            fetch_piece(k + AHEAD - 1)

        eig_copy(k).wait()
        for q in range(count):
            query_copy(k, q).wait()
        slot, start = 1, lax.rem(k, AHEAD) * piece

        def strip_of(r, carry):
            at = pl.ds(pl.multiple_of(start + r * strip, strip), strip)
            scale = 1.0 / (basis[slot, at].astype(F32) + DAMPING)
            for q in range(count):
                here = pl.ds(pl.multiple_of(q * width + k * piece + r * strip, strip), strip)
                pre[here] = (pre[here].astype(F32) * scale).astype(BF16)
            return carry

        lax.fori_loop(0, piece // strip, strip_of, 0)

    for k in range(EARLY):
        precondition(k)
    met()

    def swap(d):
        to = lax.rem(w + d, wide)
        return remote(
            grads.at[:, part_cols(to, part)], rows_held.at[held_rows(w), held_cols(part)],
            a2a_s.at[0], a2a_r.at[d], {"wide": to},
        )

    def part_copy(j):
        return remote(
            rows_held.at[:, held_cols(part)], rows_held.at[:, held_cols(part)],
            part_s.at[0], part_r.at[j - 1], {"narrow": base + lax.rem(part + j, parts)},
        )

    def own_line(c, up):
        to = wo + 1 if up else wo - 1
        slot = lookup(rank, to, wo)
        return remote(
            acts.at[:, cut(c)], acts_all.at[rows(slot, wi), cut(c)], up_s.at[int(up)], z_r.at[slot, c], line_at(to)
        )

    def line_wait(s, c):
        return remote(
            acts.at[:, cut(c)], acts_all.at[rows(s, wi), cut(c)], fwd_s.at[s], z_r.at[s, c], line_at(wo)
        )

    def onward(s):
        above = slot_plane[s] > wo
        to = jnp.where(above, wo - 1, wo + 1)
        return to, jnp.logical_and(to >= 0, to < outer)

    def forward(s, c):
        to, _ = onward(s)
        slot = lookup(rank, to, slot_plane[s])
        return remote(
            acts_all.at[rows(s, wi), cut(c)], acts_all.at[rows(slot, wi), cut(c)],
            fwd_s.at[s], z_r.at[slot, c], line_at(to),
        )

    def side_copy(e, s, c):
        source = acts.at[:, cut(c)] if s == 0 else acts_all.at[rows(s, wi), cut(c)]
        return remote(source, acts_all.at[rows(s, wi), cut(c)], y_s.at[e - 1, s], y_r.at[e - 1, s, c], side_peer(e))

    bent = DETOUR if inner == 2 else 0
    amid = jnp.logical_and(wo > 0, wo < outer - 1)

    def arrive(s, c):
        line_wait(s, c).wait_recv()
        _, more = onward(s)

        @pl.when(more)
        def _():
            forward(s, c).start()

    other = 1 - wi

    def detour(s, c):
        if s == 0:
            to, source = jnp.where(wo == 0, 1, outer - 2), wo
        else:
            (to, _), source = onward(s), slot_plane[s]
        slot = lookup(rank, to, source)
        return remote(
            acts_all.at[rows(s, other), cut(c)], acts_all.at[rows(slot, other), cut(c)],
            x_s.at[s], x_r.at[slot - 2, c], line_at(to),
        )

    def detour_wait(s, c):
        here = acts_all.at[rows(s, other), cut(c)]
        remote(here, here, x_s.at[s], x_r.at[s - 2, c], line_at(wo)).wait_recv()

    def across_side(s, c):
        for e in range(1, inner):
            side_copy(e, s, c).start()

    for d in range(1, wide):
        swap(d).start()

    def begin(c, carry):
        for e in range(1, inner):
            side_copy(e, 0, c).start()

        @pl.when(wo + 1 < outer)
        def _():
            own_line(c, True).start()

        @pl.when(wo > 0)
        def _():
            own_line(c, False).start()

        return carry

    lax.fori_loop(0, chunks, begin, 0)

    wt = tile_of(width_out, 512)

    def grads_tile(k, carry):
        at = pl.ds(pl.multiple_of(k * wt, 128), wt)
        right = weights_out[:, at]

        def left(i):
            return rows_held[pl.ds(pl.multiple_of(i * outer * block, block), outer * block), :]

        own = jnp.dot(left(wi), right, preferred_element_type=F32)
        grads_own[:, :, at] = own.reshape(outer, block, wt)
        for e in range(1, inner):
            i = lax.rem(wi + e, inner)
            other = jnp.dot(left(i), right, preferred_element_type=F32).astype(BF16)
            grads_send[i, :, :, at] = other.reshape(outer, block, wt)
        return carry

    def first(e):
        return remote(
            grads_send.at[lax.rem(wi + e, inner)], first_recv.at[e - 1], first_s.at[e], first_r.at[e], side_peer(e)
        )

    def second(d):
        to = lax.rem(wo + d, outer)
        return remote(
            grads_send.at[wi, to], second_recv.at[d - 1], second_s.at[0], second_r.at[d - 1], line_at(to)
        )

    def partial_grads():
        fetch_out.wait()
        for j in range(1, parts):
            part_copy(j).wait_recv()
        lax.fori_loop(0, width_out // wt, grads_tile, 0)
        left(rows_held.at[:, pl.ds(0, (parts - 1) * span)], part_s.at[0])
        basis_copy(2).start()

    for k in range(EARLY, BEFORE):
        precondition(k)
    per_turn = pl.cdiv(PIECES - BEFORE, chunks - 1)

    def turn_one(c, carry):
        for j in range(per_turn):
            k = BEFORE + c * per_turn + j

            @pl.when(k < PIECES)
            def _():
                precondition(k)

            @pl.when(k == PIECES - AHEAD + 1)
            def _():
                basis_copy(0).start()

            @pl.when(k == PIECES - 1)
            def _():
                basis_copy(1).start()

        arrive(1, c)
        across_side(1, c)

        @pl.when(amid)
        def _():
            arrive(2, c)

        @pl.when(c == 0)
        def _():
            fetch_out.start()
            own_acts.start()

        if bent:

            @pl.when(jnp.logical_and(jnp.logical_not(amid), c < bent))
            def _():
                side_copy(1, 0, c).wait_recv()
                detour(0, c).start()

        @pl.when(c == max(chunks - 5, 0))
        def _():
            own_rows.wait()
            for d in range(1, wide):
                swap(d).wait_recv()
            for j in range(1, parts):
                part_copy(j).start()

        @pl.when(c == chunks - 2)
        def _():
            partial_grads()

        return carry

    lax.fori_loop(0, chunks, turn_one, 0)
    for e in range(1, inner):
        first(e).start()

    pair = 2 * plane
    ct = tile_of(columns, 1792)

    def rotate(g, c):
        i = g * chunks + c
        basis_copy(i).wait()
        slot = lax.rem(i, 3)

        def tile(k, carry):
            at = pl.ds(pl.multiple_of(k * ct, 128), ct)
            value = jnp.dot(
                acts_all[g * pair : (g + 1) * pair, cut(c)], basis[slot, :, at], preferred_element_type=F32
            )

            @pl.when(c == 0)
            def _():
                total[:, at] = value

            @pl.when(c > 0)
            def _():
                total[:, at] += value

            return carry

        lax.fori_loop(0, columns // ct, tile, 0)

        @pl.when(i + 3 < 2 * chunks)
        def _():
            basis_copy(i + 3).start()

    def relay_two(c):
        @pl.when(jnp.logical_not(amid))
        def _():
            arrive(2, c)

        straight = jnp.logical_not(jnp.logical_and(amid, c < bent))

        @pl.when(straight)
        def _():
            across_side(2, c)

        @pl.when(amid)
        def _():
            arrive(3, c)

        if bent:

            @pl.when(jnp.logical_not(straight))
            def _():
                detour_wait(2, c)
                detour(2, c).start()

    def turn_two(c, carry):
        for j in range(2):
            ahead = 2 * c + j

            @pl.when(ahead < chunks)
            def _():
                relay_two(ahead)

        @pl.when(jnp.logical_or(amid, c >= bent))
        def _():
            for e in range(1, inner):
                side_copy(e, 0, c).wait_recv()

        if bent:
            late = c - (chunks - bent)

            @pl.when(jnp.logical_and(amid, late >= 0))
            def _():
                detour_wait(3, late)
                detour(3, late).start()

        for e in range(1, inner):
            side_copy(e, 1, c).wait_recv()
        rotate(0, c)
        return carry

    own_acts.wait()
    lax.fori_loop(0, chunks, turn_two, 0)

    partner = {"narrow": nx * 2 + (1 - nc)}
    mine = pl.ds(pl.multiple_of(nc * plane, plane), plane)
    theirs = pl.ds(pl.multiple_of((1 - nc) * plane, plane), plane)
    cols = 7 if columns % 896 == 0 else 1
    cw = columns // cols
    share = plane // cross

    def lane(k):
        return pl.ds(pl.multiple_of(k * cw, 128), cw)

    def cross_peer(d):
        return {"narrow": lax.rem(nx + d, cross) * 2 + nc}

    def core_copy(g):
        return remote(total.at[theirs], core_recv, core_s.at[g], core_r.at[g], partner)

    def cross_copy(d):
        to = lax.rem(nx + d, cross)
        return remote(
            core_recv.at[pl.ds(pl.multiple_of(to * share, share), share)],
            cross_recv.at[d - 1], cross_s.at[d], cross_r.at[d], cross_peer(d),
        )

    def share_rows(x):
        return pl.ds(pl.multiple_of(nc * plane + x * share, share), share)

    def done_copy(d):
        here = acts_done.at[share_rows(nx)]
        return remote(here, here, done_s.at[d], done_r.at[d], cross_peer(d))

    def last_copy(d):
        here = acts_done.at[share_rows(lax.rem(nx + cross - d, cross))]
        return remote(here, here, share_s.at[d], share_r.at[d], partner)

    def part_of(x):
        return pl.ds(pl.multiple_of(nc * plane + x * share, share), share)

    def late_rows(x):
        return pl.ds(pl.multiple_of((2 + nc) * plane + x * share, share), share)

    def late_copy(d, k):
        return remote(
            total.at[part_of(lax.rem(nx + d, cross)), lane(k)], cross_recv.at[d - 1, :, lane(k)],
            late_s.at[d - 1], late_r.at[d - 1, k], cross_peer(d),
        )

    def late_spread(d, k):
        here = acts_done.at[late_rows(nx), lane(k)]
        return remote(here, here, spread_s.at[d - 1], spread_r.at[d - 1, k], cross_peer(d))

    def late_share(d, k):
        here = acts_done.at[late_rows(lax.rem(nx + cross - d, cross)), lane(k)]
        return remote(here, here, lshare_s.at[d], lshare_r.at[d, k], partner)

    core_copy(0).start()
    core_copy(0).wait_recv()

    def core_sum(k, carry):
        core_recv[:, lane(k)] += total[mine, lane(k)]
        return carry

    lax.fori_loop(0, cols, core_sum, 0)
    for d in range(1, cross):
        cross_copy(d).start()

    def turn_three(c, carry):
        @pl.when(jnp.logical_not(amid))
        def _():
            arrive(3, c)

        @pl.when(c >= bent)
        def _():
            across_side(3, c)

        return carry

    lax.fori_loop(0, chunks, turn_three, 0)

    for e in range(1, inner):
        first(e).wait_recv()
    for o in range(outer):
        value = grads_own[o]
        for e in range(1, inner):
            value = value + first_recv[e - 1, o].astype(F32)
        grads_own[o] = value
        grads_send[wi, o] = value.astype(BF16)
    for d in range(1, outer):
        second(d).start()

    def group_shares():
        for d in range(1, cross):
            cross_copy(d).wait()
        here = pl.ds(pl.multiple_of(nx * share, share), share)

        def cross_sum(k, carry):
            value = core_recv[here, lane(k)]
            for d in range(1, cross):
                value = value + cross_recv[d - 1, :, lane(k)]
            acts_done[share_rows(nx), lane(k)] = value.astype(BF16)
            return carry

        lax.fori_loop(0, cols, cross_sum, 0)
        for d in range(1, cross):
            done_copy(d).start()
        last_copy(0).start()

    def group_done():
        for d in range(1, cross):
            done_copy(d).wait_recv()
            last_copy(d).start()

    def gline(d):
        to = lax.rem(wo + d, outer)
        slot = lookup(rank, to, wo)
        return remote(grads_all.at[0, wi], grads_all.at[slot, wi], gz_s.at[0], gz_r.at[slot], line_at(to))

    def gline_wait(s):
        return remote(grads_all.at[0, wi], grads_all.at[s, wi], gz_s.at[0], gz_r.at[s], line_at(wo))

    def gside(e, s):
        return remote(
            grads_all.at[s, wi], grads_all.at[s, wi], gy_s.at[e - 1], gy_r.at[e - 1, s], side_peer(e)
        )

    core_copy(0).wait_send()

    def grads_done():
        for d in range(1, outer):
            second(d).wait_recv()
        value = grads_own[wo]
        for d in range(1, outer):
            value = value + second_recv[d - 1].astype(F32)
        grads_all[0, wi] = value.astype(BF16)

        for d in range(1, outer):
            gline(d).start()
        for e in range(1, inner):
            gside(e, 0).start()

    def turn_four(c, carry):
        @pl.when(jnp.logical_not(jnp.logical_and(amid, c < bent)))
        def _():
            for e in range(1, inner):
                side_copy(e, 2, c).wait_recv()

        @pl.when(c >= bent)
        def _():
            for e in range(1, inner):
                side_copy(e, 3, c).wait_recv()

        if bent:

            @pl.when(jnp.logical_and(jnp.logical_not(amid), c < bent))
            def _():
                detour_wait(3, c)

        rotate(1, c)

        @pl.when(c == jnp.where(amid, chunks // 2 + 1, chunks // 2 - 1))
        def _():
            group_shares()

        @pl.when(c == jnp.where(amid, chunks // 2 + 1, chunks - 2))
        def _():
            grads_done()

        return carry

    lax.fori_loop(0, chunks, turn_four, 0)
    group_done()
    last_copy(0).wait_recv()
    core_copy(1).start()

    def grads_across(s):
        gline_wait(s).wait_recv()
        for e in range(1, inner):
            gside(e, s).start()

    core_copy(1).wait_recv()

    def late_sum(k, carry):
        value = total[mine, lane(k)] + core_recv[:, lane(k)]
        total[mine, lane(k)] = value
        for d in range(1, cross):
            late_copy(d, k).start()
        return carry

    lax.fori_loop(0, cols, late_sum, 0)
    for s in range(1, outer):
        grads_across(s)

    lanes[...] = jnp.zeros_like(lanes)

    def mix(g, k):
        left = grads_all[2 * g : 2 * g + 2].reshape(pair, width)
        here = slice(g * pair, (g + 1) * pair)
        for q in range(count):
            mixed = jnp.dot(left, pre[q * width : (q + 1) * width, lane(k)], preferred_element_type=F32)
            right = acts_done[here, lane(k)].astype(F32)
            value = jnp.zeros((pair, 128), F32)
            for j in range(cw // 128):
                value = value + mixed[:, j * 128 : (j + 1) * 128] * right[:, j * 128 : (j + 1) * 128]
            for h in range(2):
                there = pl.ds(pl.multiple_of(slot_plane[2 * g + h] * plane, plane), plane)
                lanes[q, there] += value[h * plane : (h + 1) * plane]

    def late_add(k):
        for d in range(1, cross):
            late_copy(d, k).wait_recv()
        value = total[part_of(nx), lane(k)]
        for d in range(1, cross):
            value = value + cross_recv[d - 1, :, lane(k)]
        acts_done[late_rows(nx), lane(k)] = value.astype(BF16)
        for d in range(1, cross):
            late_spread(d, k).start()
        late_share(0, k).start()

    def late_pass(k):
        for d in range(1, cross):
            late_spread(d, k).wait_recv()
            late_share(d, k).start()

    def late_lead(k, carry):
        late_add(k)
        return carry

    lead = cols // 2
    lax.fori_loop(0, lead, late_lead, 0)
    for d in range(1, cross):
        last_copy(d).wait_recv()
    for e in range(1, inner):
        for s in (0, 1):
            gside(e, s).wait_recv()

    def mix_early(k, carry):
        mix(0, k)

        @pl.when(k >= lead)
        def _():
            late_add(k)

        return carry

    lax.fori_loop(0, cols, mix_early, 0)

    for k in range(min(2, cols)):
        late_pass(k)
    for e in range(1, inner):
        for s in (2, 3):
            gside(e, s).wait_recv()

    def mix_late(k, carry):
        @pl.when(k + 2 < cols)
        def _():
            late_pass(k + 2)

        for d in range(cross):
            late_share(d, k).wait_recv()
        mix(1, k)
        return carry

    lax.fori_loop(0, cols, mix_late, 0)

    _, rows_pad, docs_pad = across.shape
    row = lax.broadcasted_iota(jnp.int32, (rows_pad, docs_pad), 0)
    value = jnp.zeros((rows_pad, docs_pad), F32)
    tokens = block * wide
    named = jnp.broadcast_to(ids[...].reshape(1, tokens), (docs_pad, tokens))
    member = (named == lax.broadcasted_iota(jnp.int32, (docs_pad, tokens), 0)).astype(F32)
    for q in range(count):
        doc_lanes = jnp.dot(member, lanes[q], precision=lax.Precision.HIGHEST, preferred_element_type=F32)
        value = jnp.where(row == q, jnp.sum(doc_lanes, axis=1)[None, :], value)
    across[n] = value

    def over_narrow(d):
        return remote(across.at[n], across.at[n], send_n.at[0], recv_n.at[d], {"narrow": lax.rem(n + d, narrow)})

    def over_wide(d):
        return remote(held.at[w], held.at[w], send_w.at[0], recv_w.at[d], {"wide": lax.rem(w + d, wide)})

    for d in range(1, narrow):
        over_narrow(d).start()
    for d in range(1, narrow):
        over_narrow(d).wait_recv()
    value = across[0]
    for d in range(1, narrow):
        value = value + across[d]
    held[w] = value
    for d in range(1, wide):
        over_wide(d).start()
    for d in range(1, wide):
        over_wide(d).wait_recv()
    value = held[0]
    for d in range(1, wide):
        value = value + held[d]
    out[...] = value[: out.shape[0], : out.shape[1]]

    left(rows_held.at[pl.ds(0, (wide - 1) * block), held_cols(0)], a2a_s.at[0])
    row_block = acts_all.at[rows(0, wi)]

    @pl.when(wo + 1 < outer)
    def _():
        left(row_block, up_s.at[1])

    @pl.when(wo > 0)
    def _():
        left(row_block, up_s.at[0])

    for s in range(1, outer):
        _, more = onward(s)

        @pl.when(more)
        def _():
            left(row_block, fwd_s.at[s])

    for e in range(1, inner):
        for s in (0, 1):
            left(row_block, y_s.at[e - 1, s])
        short = acts_all.at[rows(0, wi), pl.ds(0, (chunks - bent) * depth)]
        left(short, y_s.at[e - 1, 3])

        @pl.when(amid)
        def _():
            left(short, y_s.at[e - 1, 2])

        @pl.when(jnp.logical_not(amid))
        def _():
            left(row_block, y_s.at[e - 1, 2])

    if bent:
        long = acts_all.at[rows(0, wi), pl.ds(0, bent * depth)]

        @pl.when(amid)
        def _():
            left(long, x_s.at[2])
            left(long, x_s.at[3])

        @pl.when(jnp.logical_not(amid))
        def _():
            left(long, x_s.at[0])

    for e in range(1, inner):
        first(e).wait_send()
        left(grads_all.at[:, 0], gy_s.at[e - 1])
    left(second_recv, second_s.at[0])
    left(second_recv, gz_s.at[0])
    core_copy(1).wait_send()
    for d in range(cross):
        last_copy(d).wait_send()
    for d in range(1, cross):
        done_copy(d).wait_send()
    f32_part, bf16_part = total.at[pl.ds(0, share)], acts_done.at[pl.ds(0, share)]
    left(bf16_part, lshare_s.at[0])
    for d in range(1, cross):
        left(f32_part, late_s.at[d - 1])
        left(bf16_part, spread_s.at[d - 1])
        left(bf16_part, lshare_s.at[d])
    left(across.at[pl.ds(0, narrow - 1)], send_n.at[0])
    left(held.at[pl.ds(0, wide - 1)], send_w.at[0])


def score(wide, narrow, activations, out_grads, basis_in, basis_out, eigenvalues, queries, doc_ids):
    outer, inner = grid_of(wide)
    cross = narrow // 2
    block, depth_all = activations.shape
    tokens = block * wide
    plane = block * inner
    docs = DOC_PER * wide
    depth = tile_of(depth_all, 1024)
    chunks = depth_all // depth
    columns = basis_in.shape[1]
    rows_out, width_out = basis_out.shape
    count, width, _ = queries.shape
    cols = 7 if columns % 896 == 0 else 1
    parts = parts_of(rows_out, narrow)
    inside = fits(depth, columns, tokens, rows_out, width_out)
    rows_pad, docs_pad = pl.cdiv(count, 8) * 8, pl.cdiv(docs, 128) * 128
    dma = pltpu.SemaphoreType.DMA
    scores = pl.pallas_call(
        functools.partial(score_kernel, wide, narrow, docs),
        out_shape=jax.ShapeDtypeStruct((count, docs), F32),
        in_specs=[ANY] * 6 + [pl.BlockSpec(memory_space=pltpu.VMEM)],
        out_specs=pl.BlockSpec(memory_space=pltpu.VMEM),
        scratch_shapes=[
            pltpu.VMEM((count * width, columns), BF16),
            pltpu.VMEM((3, depth, columns), BF16),
            pltpu.VMEM((tokens, depth_all), BF16),
            pltpu.VMEM((2 * plane, columns), F32),
            pltpu.VMEM((tokens, columns), BF16),
            pltpu.VMEM((plane, columns), F32),
            pltpu.VMEM((cross - 1, plane // cross, columns), F32),
            pltpu.VMEM((16, 128) if inside else (tokens, rows_out), BF16),
            pltpu.VMEM((16, 128) if inside else (rows_out, width_out), BF16),
            pltpu.VMEM((outer, block, width_out), F32),
            pltpu.VMEM((inner, outer, block, width_out), BF16),
            pltpu.VMEM((inner - 1, outer, block, width_out), BF16),
            pltpu.VMEM((outer - 1, block, width_out), BF16),
            pltpu.VMEM((outer, inner, block, width_out), BF16),
            pltpu.VMEM((count, tokens, 128), F32),
            pltpu.VMEM((wide, rows_pad, docs_pad), F32),
            pltpu.VMEM((narrow, rows_pad, docs_pad), F32),
            dma((1,)),
            dma((1,)),
            dma((AHEAD,)),
            dma((AHEAD, count,)),
            dma((3,)),
            dma((1,)),
            dma((1,)),
            dma((wide,)),
            dma((1,)),
            dma((parts,)),
            dma((2,)),
            dma((outer,)),
            dma((outer, chunks)),
            dma((outer,)),
            dma((2, max(DETOUR, 1))),
            dma((inner - 1, outer,)),
            dma((inner - 1, outer, chunks,)),
            dma((inner,)),
            dma((inner,)),
            dma((1,)),
            dma((outer,)),
            dma((1,)),
            dma((outer,)),
            dma((inner,)),
            dma((inner - 1, outer)),
            dma((2,)),
            dma((2,)),
            dma((cross,)),
            dma((cross,)),
            dma((cross - 1,)),
            dma((cross - 1, cols)),
            dma((cross - 1,)),
            dma((cross - 1, cols)),
            dma((cross,)),
            dma((cross,)),
            dma((cross,)),
            dma((cross,)),
            dma((cross,)),
            dma((cross, cols)),
            dma((1,)),
            dma((wide,)),
            dma((1,)),
            dma((narrow,)),
        ],
        compiler_params=pltpu.CompilerParams(
            collective_id=0, has_side_effects=True, vmem_limit_bytes=VMEM_LIMIT
        ),
        name="score",
    )(activations, out_grads, basis_in, basis_out, eigenvalues, queries, doc_ids)
    return scores.T


def solution(mesh):
    wide, narrow = mesh.shape["wide"], mesh.shape["narrow"]

    def shards(activations, out_grads, basis_in, basis_out, eigenvalues, queries, doc_ids):
        return score(
            wide, narrow, activations, out_grads, basis_in, basis_out, eigenvalues, queries, doc_ids
        )

    return jax.shard_map(
        shards,
        mesh=mesh,
        in_specs=(
            P("wide", "narrow"),
            P("wide", None),
            P("narrow", "wide"),
            P("wide", "narrow"),
            P("narrow", "wide"),
            P(None, "narrow", "wide"),
            P(),
        ),
        out_specs=P(),
        check_vma=False,
    )
```
